32 devices in a mesh: groups: 2 (over x), queue: 16 (over z, y, core).
Axes of the slice: x: 2, y: 2, z: 4, core: 2. Of those that a mesh axis runs over, the one named last changes fastest.
Arguments:
- hidden: bfloat16 [256, 5120], P(('groups', 'queue')), parts along dimension 0, may hold values from -6 to 6
- incoming: bfloat16 [2, 16, 5120], P(None, 'groups'), parts along dimension 1, may hold values from -6 to 6
- levels: int32 [16], replicated, may hold values from 0 to 95, as said below
- mod_table: bfloat16 [96, 3, 5120], replicated, may hold values from -3 to 3
- query_weight: bfloat16 [5120, 5120], P(None, 'queue'), may hold values from -0.078125 to 0.078125
- key_weight: bfloat16 [5120, 5120], P(None, 'queue'), may hold values from -0.078125 to 0.078125
- value_weight: bfloat16 [5120, 5120], P(None, 'queue'), may hold values from -0.078125 to 0.078125
- output_weight: bfloat16 [5120, 5120], P(None, 'queue'), may hold values from -0.078125 to 0.078125
- query_gain: float32 [5120], replicated, may hold values from 0.5 to 1.5
- key_gain: float32 [5120], replicated, may hold values from 0.5 to 1.5
- text_keys: bfloat16 [1024, 5120], P(('groups', 'queue')), parts along dimension 0, may hold values from -6 to 6
- text_values: bfloat16 [1024, 5120], P(('groups', 'queue')), parts along dimension 0, may hold values from -6 to 6
Outputs:
- updated: bfloat16 [256, 5120], P(('groups', 'queue')), parts along dimension 0
The draws below stay inside these ranges and needn't reach their ends.
There are 2 independent parts, one for each index of `groups`. The reference program is written for one: setup_inputs(seed, part) draws one part's arguments, and reference() takes and returns one part's arrays. A program takes and returns all parts, laid end to end along the dimension named above; an argument that names none is the same for every part. Nothing has to cross between parts.
Inputs may be any that keep to these rules, and one draw needn't show every extreme that they name: `levels`: strictly rising along the queue positions; the last position always has level 95.
All inputs are finite; a program needn't handle non-finite values.
Results may differ from the reference program's by a relative error of at most 0.0085.
Values may be sent and summed in bfloat16 or wider, within the bound.
A program may use at most 128 MiB of HBM per device.

```python
import math
import jax
import jax.numpy as jnp
from jax import lax

D = 5120
HEADS = 40
HD = 128
TOK_DEV = 8
STEPS = 2
LEVELS = 96
TEXT = 512
SPANS = 16
TOKENS = 128


def draw_levels(key, part):
    order = jax.random.permutation(key, LEVELS - 1)
    picked = jnp.sort(order[:SPANS - 1])
    return jnp.concatenate([picked, jnp.array([LEVELS - 1])]).astype(jnp.int32)


def block_levels(own_key, extent, cuts, low, top_value):
    gain = 1.0
    for dim, parts in cuts:
        heights = jax.random.uniform(jax.random.fold_in(jax.random.fold_in(own_key, 6), dim), (parts,), jnp.float32, low / len(cuts), top_value / len(cuts))
        gain = gain * jnp.repeat(jnp.exp(heights), extent[dim] // parts).reshape((-1,) + (1,) * (len(extent) - 1 - dim))
    return gain


def normal_values(key, extent, deviation, most, cuts=(), held_as=jnp.bfloat16):
    drawn = jax.random.normal(key, extent, jnp.float32) * deviation
    if len(cuts) > 0:
        drawn = block_levels(key, extent, cuts, -0.22, 0.18) * drawn
    return jnp.clip(drawn, min=-most, max=most).astype(held_as)


def setup_inputs(seed: int = 0, part: int = 0) -> dict:
    key_list = jax.random.split(jax.random.key(seed), 13)
    part_splits = jax.random.split(jax.random.fold_in(key_list[12], part), 13)
    return {
        "hidden": normal_values(part_splits[0], (TOKENS, D), 1.0, 6.0, ((0, 16),)),
        "incoming": normal_values(part_splits[1], (STEPS, TOK_DEV, D), 1.0, 6.0),
        "levels": draw_levels(jax.random.fold_in(key_list[12], 71), part),
        "mod_table": normal_values(key_list[3], (LEVELS, 3, D), 0.5, 3.0),
        "query_weight": normal_values(key_list[4], (D, D), D ** -0.5, 0.078125, ((1, 16),)),
        "key_weight": normal_values(key_list[5], (D, D), D ** -0.5, 0.078125, ((1, 16),)),
        "value_weight": normal_values(key_list[6], (D, D), D ** -0.5, 0.078125, ((1, 16),)),
        "output_weight": normal_values(key_list[7], (D, D), D ** -0.5, 0.078125, ((1, 16),)),
        "query_gain": jnp.clip(1.0 + 0.1 * jax.random.normal(key_list[8], (D,), jnp.float32), 0.5, 1.5),
        "key_gain": jnp.clip(1.0 + 0.1 * jax.random.normal(key_list[9], (D,), jnp.float32), 0.5, 1.5),
        "text_keys": normal_values(part_splits[10], (TEXT, D), 1.0, 6.0, ((0, 16),)),
        "text_values": normal_values(part_splits[11], (TEXT, D), 1.0, 6.0, ((0, 16),)),
    }


def normalize(values):
    return values * lax.rsqrt(lax.optimization_barrier(jnp.mean(values * values, axis=-1, keepdims=True)) + 1e-06)

def softmax_rounded(scores):
    row_max = lax.optimization_barrier(jnp.max(scores, axis=-1, keepdims=True))
    weights = jnp.exp(scores - row_max)
    return (weights / lax.optimization_barrier(jnp.sum(weights, axis=-1, keepdims=True))).astype(jnp.bfloat16)

def reference(hidden, incoming, levels, mod_table, query_weight, key_weight, value_weight, output_weight, query_gain, key_gain, text_keys, text_values):
    modulation = jnp.take(mod_table, levels.astype(jnp.int32), axis=0).astype(jnp.float32)[:, None]
    score_scale = 1.0 / math.sqrt(HD)
    total_rows = SPANS * TOK_DEV
    span_of = (jnp.arange(total_rows) // TOK_DEV).astype(jnp.int32)
    allowed = span_of[:, None] >= span_of[None, :]
    text_k = text_keys.reshape(TEXT, HEADS, HD).transpose(1, 0, 2)
    text_v = text_values.reshape(TEXT, HEADS, HD).transpose(1, 0, 2)

    def one_head(operands):
        q_one, k_one, v_one, tk_one, tv_one = operands
        scores = jnp.dot(q_one, k_one.T, preferred_element_type=jnp.float32) * score_scale
        scores = jnp.where(allowed, scores, -1e+30)
        attended = jnp.dot(softmax_rounded(scores), v_one, preferred_element_type=jnp.float32).astype(jnp.bfloat16)
        text_scores = jnp.dot(q_one, tk_one.T, preferred_element_type=jnp.float32) * score_scale
        crossed = jnp.dot(softmax_rounded(text_scores), tv_one, preferred_element_type=jnp.float32).astype(jnp.bfloat16)
        return (attended.astype(jnp.float32) + crossed.astype(jnp.float32)).astype(jnp.bfloat16)
    queue_state = hidden
    for section_index in range(STEPS):
        queue_state = jnp.concatenate([incoming[section_index], queue_state[:-TOK_DEV]], axis=0)
        current = queue_state.astype(jnp.float32).reshape(SPANS, TOK_DEV, D)
        modulated = (normalize(current) * (1.0 + modulation[:, :, 1]) + modulation[:, :, 0]).astype(jnp.bfloat16)
        modulated = modulated.reshape(total_rows, D)
        query_rows = (normalize(jnp.dot(modulated, query_weight, preferred_element_type=jnp.float32)) * query_gain).astype(jnp.bfloat16)
        key_rows = (normalize(jnp.dot(modulated, key_weight, preferred_element_type=jnp.float32)) * key_gain).astype(jnp.bfloat16)
        value_rows = jnp.dot(modulated, value_weight, preferred_element_type=jnp.float32).astype(jnp.bfloat16)
        query_heads = query_rows.reshape(total_rows, HEADS, HD).transpose(1, 0, 2)
        key_heads = key_rows.reshape(total_rows, HEADS, HD).transpose(1, 0, 2)
        value_heads = value_rows.reshape(total_rows, HEADS, HD).transpose(1, 0, 2)
        combined = lax.map(one_head, (query_heads, key_heads, value_heads, text_k, text_v))
        combined = combined.transpose(1, 0, 2).reshape(total_rows, D)
        projected = jnp.dot(combined, output_weight, preferred_element_type=jnp.float32).reshape(SPANS, TOK_DEV, D)
        queue_state = (current + modulation[:, :, 2] * projected).astype(jnp.bfloat16).reshape(total_rows, D)
    return queue_state
```

```python
import functools
import math

import jax
import jax.numpy as jnp
from jax import lax
from jax.experimental import pallas as pl
from jax.experimental.pallas import tpu as pltpu
from jax.sharding import PartitionSpec as P

HEADS = 40
STEPS = 2
FIRST_CHUNKS = 2
CHUNKS = 2


def passed_along(value, axis, steps):
    count = lax.axis_size(axis)
    initial, last = (max(0, -steps), min(count, count - steps))
    return lax.ppermute(value, axis, [(source, source + steps) for source in range(initial, last)])


def normalize(values):
    return values * lax.rsqrt(jnp.mean(values * values, axis=-1, keepdims=True) + 1e-06)


def softmax_rounded(scores):
    row_max = jnp.max(scores, axis=-1, keepdims=True)
    weights = jnp.exp(scores - row_max)
    return (weights / jnp.sum(weights, axis=-1, keepdims=True)).astype(jnp.bfloat16)


def pad_slots(values, slot_total):
    missing = slot_total - values.shape[1]
    filler = jnp.zeros((values.shape[0], missing, values.shape[2]), values.dtype)
    return jnp.concatenate([values, filler], axis=1)


def causal_block(queries, keys_all, values_all, span_rows, score_scale):
    total_rows = queries.shape[0]
    block_rows = min(512, total_rows)
    scores = (
        jnp.einsum("qsd,ksd->sqk", queries, keys_all, preferred_element_type=jnp.float32)
        * score_scale
    )
    allowed = (
        jnp.arange(0, block_rows)[:, None] // span_rows
        >= jnp.arange(block_rows)[None, :] // span_rows
    )
    scores = jnp.where(allowed[None], scores, -1e30)
    result = jnp.einsum(
        "sqk,ksd->qsd", softmax_rounded(scores), values_all, preferred_element_type=jnp.float32
    )
    pieces = result.astype(jnp.bfloat16)
    return pieces


def text_attend(queries, text_k, text_v, score_scale):
    scores = (
        jnp.einsum("qsd,tsd->sqt", queries, text_k, preferred_element_type=jnp.float32)
        * score_scale
    )
    return jnp.einsum(
        "sqt,tsd->qsd", softmax_rounded(scores), text_v, preferred_element_type=jnp.float32
    ).astype(jnp.bfloat16)


def per_device(
    hidden,
    incoming,
    levels,
    mod_table,
    query_weight,
    key_weight,
    value_weight,
    output_weight,
    query_gain,
    key_gain,
    text_keys,
    text_values,
):
    own_index = lax.axis_index("queue")
    queue_size = lax.axis_size("queue")
    span_rows, model_width = hidden.shape
    head_size = model_width // HEADS
    score_scale = 1.0 / math.sqrt(head_size)
    slot_total = -(-HEADS // queue_size) * queue_size
    own_level = lax.dynamic_index_in_dim(levels, own_index, 0, keepdims=False)
    modulation = lax.dynamic_index_in_dim(mod_table, own_level, 0, keepdims=False).astype(
        jnp.float32
    )
    stacked_weights = jnp.stack([query_weight, key_weight, value_weight])
    text_local = text_keys.shape[0]
    text_k_slots, text_v_slots = (
        lax.all_to_all(
            pad_slots(text_keys.reshape(text_local, HEADS, head_size), slot_total),
            "queue",
            split_axis=1,
            concat_axis=0,
            tiled=True,
        ),
        lax.all_to_all(
            pad_slots(text_values.reshape(text_local, HEADS, head_size), slot_total),
            "queue",
            split_axis=1,
            concat_axis=0,
            tiled=True,
        ),
    )
    queue_state = hidden
    for section_index in range(STEPS):
        shifted = passed_along(queue_state, "queue", 1)
        queue_state = jnp.where(own_index == 0, incoming[section_index], shifted)
        current = queue_state.astype(jnp.float32)
        modulated = (normalize(current) * (1.0 + modulation[1]) + modulation[0]).astype(
            jnp.bfloat16
        )
        columns = jnp.einsum(
            "rd,cdw->crw",
            lax.all_gather(modulated, "queue", axis=0, tiled=True),
            stacked_weights,
            preferred_element_type=jnp.float32,
        )
        own_rows = lax.all_to_all(
            columns.astype(jnp.bfloat16), "queue", split_axis=1, concat_axis=2, tiled=True
        ).astype(columns.dtype)
        query_heads = (
            (normalize(own_rows[0]) * query_gain)
            .astype(jnp.bfloat16)
            .reshape(span_rows, HEADS, head_size)
        )
        key_heads = (
            (normalize(own_rows[1]) * key_gain)
            .astype(jnp.bfloat16)
            .reshape(span_rows, HEADS, head_size)
        )
        value_heads = own_rows[2].astype(jnp.bfloat16).reshape(span_rows, HEADS, head_size)
        query_slots, key_slots, value_slots = (
            lax.all_to_all(
                pad_slots(query_heads, slot_total), "queue", split_axis=1, concat_axis=0, tiled=True
            ),
            lax.all_to_all(
                pad_slots(key_heads, slot_total), "queue", split_axis=1, concat_axis=0, tiled=True
            ),
            lax.all_to_all(
                pad_slots(value_heads, slot_total), "queue", split_axis=1, concat_axis=0, tiled=True
            ),
        )
        attended_slots = causal_block(query_slots, key_slots, value_slots, span_rows, score_scale)
        crossed_slots = text_attend(query_slots, text_k_slots, text_v_slots, score_scale)
        attended_back, crossed_back = (
            lax.all_to_all(attended_slots, "queue", split_axis=0, concat_axis=1, tiled=True),
            lax.all_to_all(crossed_slots, "queue", split_axis=0, concat_axis=1, tiled=True),
        )
        attended = attended_back[:, :HEADS]
        crossed = crossed_back[:, :HEADS]
        combined = (
            (attended.astype(jnp.float32) + crossed.astype(jnp.float32))
            .astype(jnp.bfloat16)
            .reshape(span_rows, model_width)
        )
        out_columns = jnp.dot(
            lax.all_gather(combined, "queue", axis=0, tiled=True),
            output_weight,
            preferred_element_type=jnp.float32,
        )
        projected = lax.all_to_all(
            out_columns.astype(jnp.bfloat16), "queue", split_axis=0, concat_axis=1, tiled=True
        ).astype(out_columns.dtype)
        queue_state = (current + modulation[2] * projected).astype(jnp.bfloat16)
    return queue_state


def dot_nt(a, b):
    return lax.dot_general(a, b, (((1,), (1,)), ((), ())), preferred_element_type=jnp.float32)


def fused_kernel(
    n,
    cols,
    hidden,
    incoming,
    levels,
    table_hbm,
    wq_hbm,
    wk_hbm,
    wv_hbm,
    wo_hbm,
    q_gain,
    k_gain,
    tkeys,
    tvals,
    out,
    table,
    mods,
    wqkv,
    wo,
    first,
    gathered,
    full,
    acc,
    shifted,
    squares,
    piece_f32,
    piece_bf16,
    oacc,
    own_cols,
    placed,
    qb,
    kb,
    vb,
    raw_self,
    raw_text,
    xsend,
    xrecv,
    ssend,
    srecv,
    tk,
    tv,
    osend,
    orecv,
    load_sems,
    gsend_sems,
    grecv_sems,
    ssend_sems,
    srecv_sems,
    xsend_sems,
    xrecv_sems,
    tsend_sems,
    trecv_sems,
    osend_sems,
    orecv_sems,
):
    me = lax.axis_index("queue")
    span, width = hidden.shape
    head = width // HEADS
    rows = n * span
    pair = 2 * cols
    local = placed.shape[1]
    blocks = gathered.shape[2]
    shared = 2 * local - pair
    step_off = pair - local
    pad = local - cols
    core = lax.rem(me, 2)
    row = lax.rem(me // 2, 2)
    depth = me // 4
    sibling = me + 1 - 2 * core
    start_col = pl.multiple_of((me // 2) * pair + core * step_off, 128)
    mid = pl.multiple_of((1 - core) * step_off, 128)
    trows = tkeys.shape[0]
    scale = 1.0 / math.sqrt(head)

    upper = depth // 2
    folded_depth = depth + upper * (3 - 2 * depth)

    def nth(k):
        x = (folded_depth, 1 - folded_depth, 2, 3)[k]
        return x + upper * (3 - 2 * x)

    along = [4 * nth(k) + 2 * row + core for k in range(4)]
    beside = [4 * nth(k) + 2 * (1 - row) + core for k in range(4)]
    across = me + 2 - 4 * row

    def flip(slot):
        return slot + 1 - 2 * core

    barrier = pltpu.get_barrier_semaphore()
    for k in range(1, n):
        pl.semaphore_signal(
            barrier,
            inc=1,
            device_id={"queue": lax.rem(me + k, n)},
            device_id_type=pl.DeviceIdType.MESH,
        )
    own = pltpu.make_async_copy(hidden, first.at[me], load_sems.at[4])
    own.start()
    own_table = pltpu.make_async_copy(table_hbm, table, load_sems.at[7])
    own_table.start()
    blank = jnp.zeros((pad, width), jnp.bfloat16)
    gap = (1 - core) * cols
    for j in range(3):
        wqkv[pl.ds(pl.multiple_of(j * local + gap, pad), pad), :] = blank
    wo[pl.ds(pl.multiple_of(gap, pad), pad), :] = blank
    loads = [
        pltpu.make_async_copy(
            s, wqkv.at[pl.ds(pl.multiple_of(j * local + core * pad, pad), cols)], load_sems.at[j]
        )
        for j, s in enumerate((wq_hbm, wk_hbm, wv_hbm))
    ]
    loads.append(
        pltpu.make_async_copy(
            wo_hbm, wo.at[pl.ds(pl.multiple_of(core * pad, pad), cols)], load_sems.at[3]
        )
    )
    own_tk = pltpu.make_async_copy(
        tkeys.at[:, pl.ds(start_col, local)], tk.at[pl.ds(me * trows, trows)], load_sems.at[5]
    )
    own_tv = pltpu.make_async_copy(
        tvals.at[:, pl.ds(start_col, local)], tv.at[pl.ds(me * trows, trows)], load_sems.at[6]
    )
    for item in loads + [own_tk, own_tv]:
        item.start()
    own.wait()
    pl.semaphore_wait(barrier, n - 1)

    pending = []

    def remote(src, dst, send, recv, target):
        return pltpu.make_async_remote_copy(
            src_ref=src,
            dst_ref=dst,
            send_sem=send,
            recv_sem=recv,
            device_id={"queue": target},
            device_id_type=pl.DeviceIdType.MESH,
        )

    def gather(view, chunks, phase, on_chip, opening=None, last_link=None):
        bank = phase % 2
        sent = []

        def copy(slot, ch, kind, target):
            return remote(
                view(slot, ch),
                view(slot, ch),
                gsend_sems.at[bank, kind, ch],
                grecv_sems.at[phase, slot, ch],
                target,
            )

        def push(slot, ch, kind, target):
            c = copy(slot, ch, kind, target)
            c.start()
            sent.append(c)

        def arrived(slot, ch):
            copy(slot, ch, 0, sibling).wait_recv()

        for ch in range(chunks):
            push(me, ch, 0, across)
        for k in range(1, 4):
            for ch in range(chunks):
                push(me, ch, k, along[k])
        for ch in range(chunks):
            push(me, ch, 4, sibling)
        if opening is not None:
            opening()

        def line(k):
            for ch in range(chunks):
                arrived(along[k], ch)
                push(along[k], ch, 4 + k, across)
                push(along[k], ch, 7 + k, sibling)

        def side(k):
            for ch in range(chunks):
                arrived(beside[k], ch)
                push(beside[k], ch, 11 + k, sibling)

        def chip(slot):
            for ch in range(chunks):
                arrived(flip(slot), ch)
            on_chip(slot // 2)

        line(1)
        chip(me)
        side(0)
        chip(along[1])
        line(2)
        chip(beside[0])
        side(1)
        chip(along[2])
        line(3)
        if last_link is not None:
            last_link()
        chip(beside[1])
        side(2)
        chip(along[3])
        side(3)
        chip(beside[2])
        chip(beside[3])

        def finish():
            for c in sent:
                c.wait_send()

        return finish

    def pack(value, dst):
        placed[...] = value
        dst[:rows, :] = placed[:, pl.ds(pl.multiple_of(core * shared, 128), step_off)].astype(
            jnp.bfloat16
        )
        half = rows // 2
        folded = placed[:half, pl.ds(mid, shared)] + pltpu.roll(
            placed[half:, pl.ds(mid, shared)], shared // 2, 1
        )
        fold = half * shared // step_off
        for e in range(step_off // shared):
            dst[rows:, e * shared : (e + 1) * shared] = folded[
                e * fold : (e + 1) * fold
            ].astype(jnp.bfloat16)

    low = lax.broadcasted_iota(jnp.int32, (rows // 2, shared), 1) < shared // 2

    def unpack(buf, chip, dst):
        a, b = buf.at[2 * chip], buf.at[2 * chip + 1]
        half = rows // 2
        dst[:, :step_off] = a[:rows, :].astype(dst.dtype)
        dst[:, local:pair] = b[:rows, :].astype(dst.dtype)
        fa, fb = (
            jnp.concatenate(
                [
                    r[rows:, e * shared : (e + 1) * shared].astype(jnp.float32)
                    for e in range(step_off // shared)
                ],
                axis=0,
            )
            for r in (a, b)
        )
        dst[:half, step_off:local] = jnp.where(low, fa, fb).astype(dst.dtype)
        dst[half:, step_off:local] = pltpu.roll(jnp.where(low, fb, fa), shared // 2, 1).astype(
            dst.dtype
        )

    lane = lax.broadcasted_iota(jnp.int32, (rows, local), 1)
    shift = core * pad
    mine = (lane >= shift) & (lane < shift + cols)

    def assemble(buf, dst, base, count):
        for p in range(n // 2):
            a = buf[2 * p, :count]
            b = buf[2 * p + 1, :count]
            at = p * pair
            kept = pl.ds(base, count)
            dst[kept, at : at + step_off] = a[:, :step_off].astype(dst.dtype)
            dst[kept, at + step_off : at + local] = (
                a[:, step_off:].astype(jnp.float32) + b[:, :shared].astype(jnp.float32)
            ).astype(dst.dtype)
            dst[kept, at + local : at + pair] = b[:, shared:].astype(dst.dtype)

    def spread(ref, at):
        return jnp.concatenate(
            [
                jnp.broadcast_to(ref[(j + 1) % n : (j + 1) % n + 1, at], (span, at.size))
                for j in range(n)
            ],
            axis=0,
        )

    qg = q_gain[:, pl.ds(start_col, local)]
    kg = k_gain[:, pl.ds(start_col, local)]
    ones = jnp.ones((8, local), jnp.float32)
    at_row = lax.broadcasted_iota(jnp.int32, (rows, rows), 0) // span
    at_col = lax.broadcasted_iota(jnp.int32, (rows, rows), 1) // span
    allowed = lax.rem(at_row + 1, n) >= lax.rem(at_col + 1, n)

    text = []

    def send_text():
        for k in range(1, n):
            target = lax.rem(me + k, n)
            col = pl.multiple_of((target // 2) * pair + lax.rem(target, 2) * step_off, 128)
            for kind, (s, d) in enumerate(((tkeys, tk), (tvals, tv))):
                c = remote(
                    s.at[:, pl.ds(col, local)],
                    d.at[pl.ds(me * trows, trows)],
                    tsend_sems.at[kind, k],
                    trecv_sems.at[kind, me],
                    target,
                )
                c.start()
                text.append(c)

    def prepare():
        own_table.wait()
        picks = (
            lax.broadcasted_iota(jnp.int32, (table.shape[1], n), 0) == levels[...]
        ).astype(jnp.float32)
        picks = jnp.transpose(picks).astype(jnp.bfloat16)
        drift, gain, gate = (
            jnp.dot(picks, table[kind], preferred_element_type=jnp.float32) for kind in range(3)
        )
        full[rows:, :] = drift.astype(jnp.bfloat16)
        mods[0] = 1.0 + gain
        mods[1] = gate

    fresh_row = lax.broadcasted_iota(jnp.int32, (2 * span, 1024), 0) >= span

    def rows_in(chip):
        at = pl.ds(pl.multiple_of(chip * 2 * span, 2 * span), 2 * span)
        fresh = fresh_row & (chip == n // 2 - 1)
        later = lax.rem(2 * chip + 2, n)
        total = jnp.zeros((2 * span, 128), jnp.float32)
        for c in range(0, width, 1024):
            block = slice(c, c + 1024)
            new = incoming[0, :, block].astype(jnp.float32)
            x = jnp.concatenate(
                [
                    first[2 * chip, :, block].astype(jnp.float32),
                    first[2 * chip + 1, :, block].astype(jnp.float32),
                ],
                axis=0,
            )
            x = jnp.where(fresh, jnp.concatenate([new, new], axis=0), x)
            gain = jnp.concatenate(
                [
                    jnp.broadcast_to(mods[0, pl.ds(s, 1), block], (span, 1024))
                    for s in (2 * chip + 1, later)
                ],
                axis=0,
            )
            full[at, block] = (x * gain).astype(jnp.bfloat16)
            y = x * x
            for e in range(0, 1024, 128):
                total = total + y[:, e : e + 128]
        squares[at, :] = total

    def columns_in(step, source):
        fresh_from = rows - span

        def on_chip(chip):
            at = pl.ds(pl.multiple_of(chip * pair, 128), pair)
            unpack(source, chip, piece_f32)
            piece_f32[fresh_from:, :] = incoming[step, :, at].astype(jnp.float32)
            x = piece_f32[...]
            piece_bf16[...] = (x * spread(mods.at[0], at)).astype(jnp.bfloat16)
            y = x * x
            total = squares[...]
            for e in range(0, pair, 128):
                total = total + y[:, e : e + 128]
            squares[...] = total
            acc[...] = acc[...] + dot_nt(piece_bf16[...], wqkv[:, at])

        return on_chip

    def features_in(source):
        def on_chip(chip):
            at = pl.ds(pl.multiple_of(chip * pair, 128), pair)
            unpack(source, chip, piece_bf16)
            oacc[...] = oacc[...] + dot_nt(piece_bf16[...], wo[:, at])

        return on_chip

    part = width // FIRST_CHUNKS
    piece = blocks // CHUNKS

    def block_view(phase):
        return lambda slot, ch: gathered.at[phase, slot, pl.ds(ch * piece, piece)]

    own_at = pl.ds(start_col, local)
    finish = gather(
        lambda slot, ch: first.at[slot, :, pl.ds(ch * part, part)],
        FIRST_CHUNKS,
        0,
        rows_in,
        prepare,
        send_text,
    )
    for step in range(STEPS):
        if step == 0:
            for item in loads[:3]:
                item.wait()
            result = dot_nt(full[...], wqkv[...])
            acc[...] = result[:rows]
            shifted[...] = result[rows:]
            for s in range(n - 1):
                own_cols[s * span : (s + 1) * span, :] = first[s, :, own_at].astype(jnp.float32)
        own_cols[rows - span :, :] = incoming[step, :, own_at].astype(jnp.float32)
        r = lax.rsqrt(
            jnp.sum(squares[...], axis=-1, keepdims=True) * (1.0 / width) + 1e-06
        )

        def projected_by(j):
            at = pl.ds(j * local, local)
            return r * acc[:, at] + spread(shifted, at)

        q = projected_by(0)
        ssend[step, 0:1] = dot_nt(ones, q * q)[0:1]
        k_ = projected_by(1)
        ssend[step, 1:2] = dot_nt(ones, k_ * k_)[0:1]
        for k in range(1, n):
            c = remote(
                ssend.at[step],
                srecv.at[step, me],
                ssend_sems.at[step, k],
                srecv_sems.at[step, me],
                lax.rem(me + k, n),
            )
            c.start()
            pending.append(c)
        qb[...] = (q * qg).astype(jnp.bfloat16)
        kb[...] = (k_ * kg).astype(jnp.bfloat16)
        xsend[step, 0] = qb[:, pl.ds(mid, shared)]
        xsend[step, 1] = kb[:, pl.ds(mid, shared)]
        swap = remote(
            xsend.at[step], xrecv.at[step], xsend_sems.at[step], xrecv_sems.at[step], sibling
        )
        swap.start()
        srecv[step, me] = ssend[step]
        vb[...] = projected_by(2).astype(jnp.bfloat16)
        swap.wait()
        qb[:, pl.ds(mid, shared)] = qb[:, pl.ds(mid, shared)] + xrecv[step, 0]
        kb[:, pl.ds(mid, shared)] = kb[:, pl.ds(mid, shared)] + xrecv[step, 1]
        for h in range(local // head):
            at = slice(h * head, (h + 1) * head)
            raw_self[h] = dot_nt(qb[:, at], kb[:, at])
        if step > 0:
            for h in range(local // head):
                at = slice(h * head, (h + 1) * head)
                raw_text[h] = dot_nt(qb[:, at], tk[:, at])
        for k in range(1, n):
            src = lax.rem(me + k, n)
            remote(
                ssend.at[step],
                srecv.at[step, src],
                ssend_sems.at[step, k],
                srecv_sems.at[step, src],
                sibling,
            ).wait_recv()
        total = jnp.sum(srecv[step], axis=0)
        inv = lax.rsqrt(total * (1.0 / width) + 1e-06)
        q_col = jnp.transpose(jnp.broadcast_to(inv[0:1], (rows, rows)))[:, 0:1] * scale
        k_row = inv[1:2]
        for h in range(local // head):
            at = slice(h * head, (h + 1) * head)
            s = raw_self[h] * q_col * k_row
            s = jnp.where(allowed, s, -1e30)
            w = jnp.exp(s - jnp.max(s, axis=-1, keepdims=True))
            placed[:, at] = jnp.dot(
                w.astype(jnp.bfloat16), vb[:, at], preferred_element_type=jnp.float32
            ) / jnp.sum(w, axis=-1, keepdims=True)
        if step == 0:
            own_tk.wait()
            own_tv.wait()
            for kind, d in enumerate((tk, tv)):
                for k in range(1, n):
                    src = lax.rem(me + k, n)
                    remote(
                        d.at[pl.ds(src * trows, trows)],
                        d.at[pl.ds(src * trows, trows)],
                        tsend_sems.at[kind, k],
                        trecv_sems.at[kind, src],
                        sibling,
                    ).wait_recv()
                if kind == 0:
                    for h in range(local // head):
                        at = slice(h * head, (h + 1) * head)
                        raw_text[h] = dot_nt(qb[:, at], tk[:, at])
        parts = []
        for h in range(local // head):
            at = slice(h * head, (h + 1) * head)
            t = raw_text[h] * q_col
            w = jnp.exp(t - jnp.max(t, axis=-1, keepdims=True))
            b = jnp.dot(
                w.astype(jnp.bfloat16), tv[:, at], preferred_element_type=jnp.float32
            ) / jnp.sum(w, axis=-1, keepdims=True)
            parts.append(placed[:, at] + b)
        pack(
            jnp.where(mine, jnp.concatenate(parts, axis=1), 0.0), gathered.at[2 * step, me]
        )
        finish()
        oacc[...] = jnp.zeros_like(oacc)
        if step == 0:
            loads[3].wait()
        finish = gather(
            block_view(2 * step), CHUNKS, 2 * step + 1, features_in(gathered.at[2 * step])
        )
        state = jnp.where(
            mine, own_cols[...] + spread(mods.at[1], own_at) * oacc[...], 0.0
        )
        state = jnp.concatenate([state[rows - span :], state[: rows - span]], axis=0)
        if step < STEPS - 1:
            pack(state, gathered.at[2 * step + 1, me])
            finish()
            own_cols[...] = state.astype(jnp.bfloat16).astype(jnp.float32)
            acc[...] = jnp.zeros_like(acc)
            squares[...] = jnp.zeros_like(squares)
            finish = gather(
                block_view(2 * step + 1),
                CHUNKS,
                2 * step + 2,
                columns_in(step + 1, gathered.at[2 * step + 1]),
            )
        else:
            osend[...] = state.reshape(n, span, local).astype(jnp.bfloat16)
            for k in range(1, n):
                target = lax.rem(me + k, n)
                c = remote(
                    osend.at[target],
                    orecv.at[me],
                    osend_sems.at[k],
                    orecv_sems.at[me],
                    target,
                )
                c.start()
                pending.append(c)
            orecv[me] = osend[me]
    for k in range(1, n):
        src = lax.rem(me + k, n)
        remote(
            osend.at[src], orecv.at[src], osend_sems.at[k], orecv_sems.at[src], sibling
        ).wait_recv()
    assemble(orecv, out, 0, span)
    for c in text:
        c.wait_send()
    finish()
    for c in pending:
        c.wait_send()


def per_device_fused(
    hidden,
    incoming,
    levels,
    mod_table,
    query_weight,
    key_weight,
    value_weight,
    output_weight,
    query_gain,
    key_gain,
    text_keys,
    text_values,
):
    n = lax.axis_size("queue")
    span, width = hidden.shape
    cols = query_weight.shape[1]
    head = width // HEADS
    local = -(-cols // head) * head
    shared = 2 * local - 2 * cols
    step_off = 2 * cols - local
    pair = 2 * cols
    rows = n * span
    text = n * text_keys.shape[0]
    vmem = pl.BlockSpec(memory_space=pltpu.VMEM)
    anywhere = pl.BlockSpec(memory_space=pl.ANY)
    dma = pltpu.SemaphoreType.DMA
    bf16, f32 = jnp.bfloat16, jnp.float32
    most = max(FIRST_CHUNKS, CHUNKS)
    return pl.pallas_call(
        functools.partial(fused_kernel, n, cols),
        out_shape=jax.ShapeDtypeStruct((span, width), hidden.dtype),
        in_specs=[anywhere, vmem, vmem] + [anywhere] * 5 + [vmem] * 2 + [anywhere] * 2,
        out_specs=vmem,
        scratch_shapes=[
            pltpu.VMEM((3, mod_table.shape[0], width), bf16),
            pltpu.VMEM((2, n, width), f32),
            pltpu.VMEM((3 * local, width), bf16),
            pltpu.VMEM((local, width), bf16),
            pltpu.VMEM((n, span, width), bf16),
            pltpu.VMEM((2 * STEPS - 1, n, rows * cols // step_off, step_off), bf16),
            pltpu.VMEM((rows + n, width), bf16),
            pltpu.VMEM((rows, 3 * local), f32),
            pltpu.VMEM((n, 3 * local), f32),
            pltpu.VMEM((rows, 128), f32),
            pltpu.VMEM((rows, pair), f32),
            pltpu.VMEM((rows, pair), bf16),
            pltpu.VMEM((rows, local), f32),
            pltpu.VMEM((rows, local), f32),
            pltpu.VMEM((rows, local), f32),
            pltpu.VMEM((rows, local), bf16),
            pltpu.VMEM((rows, local), bf16),
            pltpu.VMEM((rows, local), bf16),
            pltpu.VMEM((local // head, rows, rows), f32),
            pltpu.VMEM((local // head, rows, text), f32),
            pltpu.VMEM((STEPS, 2, rows, shared), bf16),
            pltpu.VMEM((STEPS, 2, rows, shared), bf16),
            pltpu.VMEM((STEPS, 2, rows), f32),
            pltpu.VMEM((STEPS, n, 2, rows), f32),
            pltpu.VMEM((text, local), bf16),
            pltpu.VMEM((text, local), bf16),
            pltpu.VMEM((n, span, local), bf16),
            pltpu.VMEM((n, span, local), bf16),
            dma((8,)),
            dma((2, 15, most)),
            dma((2 * STEPS, n, most)),
            dma((STEPS, n)),
            dma((STEPS, n)),
            dma((STEPS,)),
            dma((STEPS,)),
            dma((2, n)),
            dma((2, n)),
            dma((n,)),
            dma((n,)),
        ],
        compiler_params=pltpu.CompilerParams(
            collective_id=0, has_side_effects=True, vmem_limit_bytes=60 * 1024 * 1024
        ),
    )(
        hidden,
        incoming,
        levels.reshape(1, n),
        mod_table.transpose(1, 0, 2),
        query_weight.T,
        key_weight.T,
        value_weight.T,
        output_weight.T,
        query_gain.reshape(1, width),
        key_gain.reshape(1, width),
        text_keys,
        text_values,
    )


def fits_fused(count, rows_total, width, groups):
    head = width // HEADS
    cols = width // count
    span = rows_total // (count * groups)
    return (
        count // 4 == 4
        and count % 4 == 0
        and width % 1024 == 0
        and head == 128
        and span == 8
        and (2 * cols) % head == 0
        and cols % head == head // 2
        and cols > head
        and count * span == 128
    )


def choose(mesh):
    def run(hidden, incoming, levels, mod_table, *rest):
        count = lax.axis_size("queue")
        if fits_fused(count, hidden.shape[0] * count, hidden.shape[1], 1):
            return per_device_fused(hidden, incoming, levels, mod_table, *rest)
        return per_device(hidden, incoming, levels, mod_table, *rest)

    return run


def solution(mesh):
    in_specs = (
        P(("groups", "queue"), None),
        P(None, "groups", None),
        P(),
        P(),
        P(None, "queue"),
        P(None, "queue"),
        P(None, "queue"),
        P(None, "queue"),
        P(),
        P(),
        P(("groups", "queue"), None),
        P(("groups", "queue"), None),
    )
    out_specs = P(("groups", "queue"), None)
    return jax.shard_map(
        choose(mesh), mesh=mesh, in_specs=in_specs, out_specs=out_specs, check_vma=False
    )
```

```python
import functools
import math

import jax
import jax.numpy as jnp
from jax import lax
from jax.experimental import pallas as pl
from jax.experimental.pallas import tpu as pltpu
from jax.sharding import PartitionSpec as P

HEADS = 40
STEPS = 2
FIRST_CHUNKS = 2
CHUNKS = 2


def passed_along(value, axis, steps):
    count = lax.axis_size(axis)
    initial, last = (max(0, -steps), min(count, count - steps))
    return lax.ppermute(value, axis, [(source, source + steps) for source in range(initial, last)])


def normalize(values):
    return values * lax.rsqrt(jnp.mean(values * values, axis=-1, keepdims=True) + 1e-06)


def softmax_rounded(scores):
    row_max = jnp.max(scores, axis=-1, keepdims=True)
    weights = jnp.exp(scores - row_max)
    return (weights / jnp.sum(weights, axis=-1, keepdims=True)).astype(jnp.bfloat16)


def pad_slots(values, slot_total):
    missing = slot_total - values.shape[1]
    filler = jnp.zeros((values.shape[0], missing, values.shape[2]), values.dtype)
    return jnp.concatenate([values, filler], axis=1)


def causal_block(queries, keys_all, values_all, span_rows, score_scale):
    total_rows = queries.shape[0]
    block_rows = min(512, total_rows)
    scores = (
        jnp.einsum("qsd,ksd->sqk", queries, keys_all, preferred_element_type=jnp.float32)
        * score_scale
    )
    allowed = (
        jnp.arange(0, block_rows)[:, None] // span_rows
        >= jnp.arange(block_rows)[None, :] // span_rows
    )
    scores = jnp.where(allowed[None], scores, -1e30)
    result = jnp.einsum(
        "sqk,ksd->qsd", softmax_rounded(scores), values_all, preferred_element_type=jnp.float32
    )
    pieces = result.astype(jnp.bfloat16)
    return pieces


def text_attend(queries, text_k, text_v, score_scale):
    scores = (
        jnp.einsum("qsd,tsd->sqt", queries, text_k, preferred_element_type=jnp.float32)
        * score_scale
    )
    return jnp.einsum(
        "sqt,tsd->qsd", softmax_rounded(scores), text_v, preferred_element_type=jnp.float32
    ).astype(jnp.bfloat16)


def per_device(
    hidden,
    incoming,
    levels,
    mod_table,
    query_weight,
    key_weight,
    value_weight,
    output_weight,
    query_gain,
    key_gain,
    text_keys,
    text_values,
):
    own_index = lax.axis_index("queue")
    queue_size = lax.axis_size("queue")
    span_rows, model_width = hidden.shape
    head_size = model_width // HEADS
    score_scale = 1.0 / math.sqrt(head_size)
    slot_total = -(-HEADS // queue_size) * queue_size
    own_level = lax.dynamic_index_in_dim(levels, own_index, 0, keepdims=False)
    modulation = lax.dynamic_index_in_dim(mod_table, own_level, 0, keepdims=False).astype(
        jnp.float32
    )
    stacked_weights = jnp.stack([query_weight, key_weight, value_weight])
    text_local = text_keys.shape[0]
    text_k_slots, text_v_slots = (
        lax.all_to_all(
            pad_slots(text_keys.reshape(text_local, HEADS, head_size), slot_total),
            "queue",
            split_axis=1,
            concat_axis=0,
            tiled=True,
        ),
        lax.all_to_all(
            pad_slots(text_values.reshape(text_local, HEADS, head_size), slot_total),
            "queue",
            split_axis=1,
            concat_axis=0,
            tiled=True,
        ),
    )
    queue_state = hidden
    for section_index in range(STEPS):
        shifted = passed_along(queue_state, "queue", 1)
        queue_state = jnp.where(own_index == 0, incoming[section_index], shifted)
        current = queue_state.astype(jnp.float32)
        modulated = (normalize(current) * (1.0 + modulation[1]) + modulation[0]).astype(
            jnp.bfloat16
        )
        columns = jnp.einsum(
            "rd,cdw->crw",
            lax.all_gather(modulated, "queue", axis=0, tiled=True),
            stacked_weights,
            preferred_element_type=jnp.float32,
        )
        own_rows = lax.all_to_all(
            columns.astype(jnp.bfloat16), "queue", split_axis=1, concat_axis=2, tiled=True
        ).astype(columns.dtype)
        query_heads = (
            (normalize(own_rows[0]) * query_gain)
            .astype(jnp.bfloat16)
            .reshape(span_rows, HEADS, head_size)
        )
        key_heads = (
            (normalize(own_rows[1]) * key_gain)
            .astype(jnp.bfloat16)
            .reshape(span_rows, HEADS, head_size)
        )
        value_heads = own_rows[2].astype(jnp.bfloat16).reshape(span_rows, HEADS, head_size)
        query_slots, key_slots, value_slots = (
            lax.all_to_all(
                pad_slots(query_heads, slot_total), "queue", split_axis=1, concat_axis=0, tiled=True
            ),
            lax.all_to_all(
                pad_slots(key_heads, slot_total), "queue", split_axis=1, concat_axis=0, tiled=True
            ),
            lax.all_to_all(
                pad_slots(value_heads, slot_total), "queue", split_axis=1, concat_axis=0, tiled=True
            ),
        )
        attended_slots = causal_block(query_slots, key_slots, value_slots, span_rows, score_scale)
        crossed_slots = text_attend(query_slots, text_k_slots, text_v_slots, score_scale)
        attended_back, crossed_back = (
            lax.all_to_all(attended_slots, "queue", split_axis=0, concat_axis=1, tiled=True),
            lax.all_to_all(crossed_slots, "queue", split_axis=0, concat_axis=1, tiled=True),
        )
        attended = attended_back[:, :HEADS]
        crossed = crossed_back[:, :HEADS]
        combined = (
            (attended.astype(jnp.float32) + crossed.astype(jnp.float32))
            .astype(jnp.bfloat16)
            .reshape(span_rows, model_width)
        )
        out_columns = jnp.dot(
            lax.all_gather(combined, "queue", axis=0, tiled=True),
            output_weight,
            preferred_element_type=jnp.float32,
        )
        projected = lax.all_to_all(
            out_columns.astype(jnp.bfloat16), "queue", split_axis=0, concat_axis=1, tiled=True
        ).astype(out_columns.dtype)
        queue_state = (current + modulation[2] * projected).astype(jnp.bfloat16)
    return queue_state


def dot_nt(a, b):
    return lax.dot_general(a, b, (((1,), (1,)), ((), ())), preferred_element_type=jnp.float32)


def fused_kernel(
    n,
    cols,
    hidden,
    incoming,
    levels,
    table_hbm,
    wq_hbm,
    wk_hbm,
    wv_hbm,
    wo_hbm,
    q_gain,
    k_gain,
    tkeys,
    tvals,
    out,
    table,
    mods,
    wqkv,
    wo,
    first,
    gathered,
    full,
    acc,
    shifted,
    squares,
    piece_f32,
    piece_bf16,
    oacc,
    own_cols,
    placed,
    qb,
    kb,
    vb,
    raw_self,
    raw_text,
    xsend,
    xrecv,
    ssend,
    srecv,
    tk,
    tv,
    tmid,
    osend,
    orecv,
    load_sems,
    gsend_sems,
    grecv_sems,
    ssend_sems,
    srecv_sems,
    xsend_sems,
    xrecv_sems,
    tsend_sems,
    trecv_sems,
    msend_sems,
    mrecv_sems,
    msib_sems,
    osend_sems,
    orecv_sems,
):
    me = lax.axis_index("queue")
    span, width = hidden.shape
    head = width // HEADS
    rows = n * span
    pair = 2 * cols
    local = placed.shape[1]
    blocks = gathered.shape[2]
    shared = 2 * local - pair
    step_off = pair - local
    pad = local - cols
    core = lax.rem(me, 2)
    row = lax.rem(me // 2, 2)
    depth = me // 4
    sibling = me + 1 - 2 * core
    start_col = pl.multiple_of((me // 2) * pair + core * step_off, 128)
    mid = pl.multiple_of((1 - core) * step_off, 128)
    mid_start = pl.multiple_of((me // 2) * pair + step_off, 128)
    own_start = pl.multiple_of((me // 2) * pair + core * local, 128)
    trows = tkeys.shape[0]
    scale = 1.0 / math.sqrt(head)

    upper = depth // 2
    folded_depth = depth + upper * (3 - 2 * depth)

    def nth(k):
        x = (folded_depth, 1 - folded_depth, 2, 3)[k]
        return x + upper * (3 - 2 * x)

    along = [4 * nth(k) + 2 * row + core for k in range(4)]
    beside = [4 * nth(k) + 2 * (1 - row) + core for k in range(4)]
    across = me + 2 - 4 * row

    def flip(slot):
        return slot + 1 - 2 * core

    barrier = pltpu.get_barrier_semaphore()
    for k in range(1, n):
        pl.semaphore_signal(
            barrier,
            inc=1,
            device_id={"queue": lax.rem(me + k, n)},
            device_id_type=pl.DeviceIdType.MESH,
        )
    own = pltpu.make_async_copy(hidden, first.at[me], load_sems.at[4])
    own.start()
    own_table = pltpu.make_async_copy(table_hbm, table, load_sems.at[7])
    own_table.start()
    blank = jnp.zeros((pad, width), jnp.bfloat16)
    gap = (1 - core) * cols
    for j in range(3):
        wqkv[pl.ds(pl.multiple_of(j * local + gap, pad), pad), :] = blank
    wo[pl.ds(pl.multiple_of(gap, pad), pad), :] = blank
    loads = [
        pltpu.make_async_copy(
            s, wqkv.at[pl.ds(pl.multiple_of(j * local + core * pad, pad), cols)], load_sems.at[j]
        )
        for j, s in enumerate((wq_hbm, wk_hbm, wv_hbm))
    ]
    loads.append(
        pltpu.make_async_copy(
            wo_hbm, wo.at[pl.ds(pl.multiple_of(core * pad, pad), cols)], load_sems.at[3]
        )
    )
    own_text = [
        pltpu.make_async_copy(
            s.at[:, pl.ds(own_start, step_off)], d.at[pl.ds(me * trows, trows)], load_sems.at[5 + i]
        )
        for i, (s, d) in enumerate(((tkeys, tk), (tvals, tv)))
    ]

    def own_middle(kind):
        return pltpu.make_async_copy(
            (tkeys, tvals)[kind].at[:, pl.ds(mid_start, shared)],
            tmid.at[kind, pl.ds(me * trows, trows)],
            load_sems.at[8],
        )

    for kind in range(2):

        @pl.when(core == kind)
        def _():
            own_middle(kind).start()

    for item in loads + own_text:
        item.start()
    own.wait()
    pl.semaphore_wait(barrier, n - 1)

    pending = []

    def remote(src, dst, send, recv, target):
        return pltpu.make_async_remote_copy(
            src_ref=src,
            dst_ref=dst,
            send_sem=send,
            recv_sem=recv,
            device_id={"queue": target},
            device_id_type=pl.DeviceIdType.MESH,
        )

    def gather(view, chunks, phase):
        bank = phase % 2
        sent = []

        def copy(slot, ch, kind, target):
            return remote(
                view(slot, ch),
                view(slot, ch),
                gsend_sems.at[bank, kind, ch],
                grecv_sems.at[phase, slot, ch],
                target,
            )

        def push(slot, ch, kind, target):
            c = copy(slot, ch, kind, target)
            c.start()
            sent.append(c)

        def arrived(slot, ch):
            copy(slot, ch, 0, sibling).wait_recv()

        def start(some):
            for ch in some:
                push(me, ch, 0, across)
            for k in range(1, 4):
                for ch in some:
                    push(me, ch, k, along[k])
            for ch in some:
                push(me, ch, 4, sibling)

        def line(k):
            for ch in range(chunks):
                arrived(along[k], ch)
                push(along[k], ch, 4 + k, across)
                push(along[k], ch, 7 + k, sibling)

        def side(k):
            for ch in range(chunks):
                arrived(beside[k], ch)
                push(beside[k], ch, 11 + k, sibling)

        def run(on_chip, late=None):
            def chip(slot, opening=False):
                for ch in range(chunks):
                    arrived(flip(slot), ch)
                on_chip(slot // 2, opening)

            line(1)
            chip(me, True)
            side(0)
            chip(along[1])
            line(2)
            chip(beside[0])
            side(1)
            chip(along[2])
            line(3)
            if late is not None:
                late()
            chip(beside[1])
            side(2)
            chip(along[3])
            side(3)
            chip(beside[2])
            chip(beside[3])

        def finish():
            for c in sent:
                c.wait_send()

        return start, run, finish

    full_heads = step_off // head
    half = rows // 2
    low = lax.broadcasted_iota(jnp.int32, (half, shared), 1) < shared // 2
    owned = (
        lax.broadcasted_iota(jnp.int32, (rows, shared), 1) // (shared // 2)
    ) == core

    def head_at(i):
        if i == full_heads:
            return pl.ds(mid, head)
        return pl.ds(pl.multiple_of(core * shared + i * head, 128), head)

    def pack(value, i, dst):
        if i < full_heads:
            dst[i * rows : (i + 1) * rows, :] = value.astype(jnp.bfloat16)
        else:
            kept = jnp.where(owned, value, 0.0)
            dst[full_heads * rows :, :] = (
                kept[:half] + pltpu.roll(kept[half:], shared // 2, 1)
            ).astype(jnp.bfloat16)

    def unpack(buf, chip, dst):
        a, b = buf.at[2 * chip], buf.at[2 * chip + 1]
        for i in range(full_heads):
            part = slice(i * rows, (i + 1) * rows)
            dst[:, i * head : (i + 1) * head] = a[part, :].astype(dst.dtype)
            dst[:, local + i * head : local + (i + 1) * head] = b[part, :].astype(dst.dtype)
        fa, fb = (r[full_heads * rows :, :].astype(jnp.float32) for r in (a, b))
        dst[:half, step_off:local] = jnp.where(low, fa, fb).astype(dst.dtype)
        dst[half:, step_off:local] = pltpu.roll(jnp.where(low, fb, fa), shared // 2, 1).astype(
            dst.dtype
        )

    lane = lax.broadcasted_iota(jnp.int32, (rows, local), 1)
    shift = core * pad
    mine = (lane >= shift) & (lane < shift + cols)

    def assemble(buf, dst, base, count):
        for p in range(n // 2):
            a = buf[2 * p, :count]
            b = buf[2 * p + 1, :count]
            at = p * pair
            kept = pl.ds(base, count)
            dst[kept, at : at + step_off] = a[:, :step_off].astype(dst.dtype)
            dst[kept, at + step_off : at + local] = (
                a[:, step_off:].astype(jnp.float32) + b[:, :shared].astype(jnp.float32)
            ).astype(dst.dtype)
            dst[kept, at + local : at + pair] = b[:, shared:].astype(dst.dtype)

    def spread(ref, at):
        return jnp.concatenate(
            [
                jnp.broadcast_to(ref[(j + 1) % n : (j + 1) % n + 1, at], (span, at.size))
                for j in range(n)
            ],
            axis=0,
        )

    qg = q_gain[:, pl.ds(start_col, local)]
    kg = k_gain[:, pl.ds(start_col, local)]
    ones = jnp.ones((8, local), jnp.float32)
    at_row = lax.broadcasted_iota(jnp.int32, (rows, rows), 0) // span
    at_col = lax.broadcasted_iota(jnp.int32, (rows, rows), 1) // span
    allowed = lax.rem(at_row + 1, n) >= lax.rem(at_col + 1, n)

    text = []

    def send_text(hops):
        for hop in hops:
            there = lax.rem(me // 2 + hop, n // 2)
            base = pl.multiple_of(there * pair, 128)
            mine_rows = pl.ds(me * trows, trows)
            copies = [
                (
                    e,
                    remote(
                        s.at[:, pl.ds(pl.multiple_of(base + step_off, 128), shared)],
                        tmid.at[e, mine_rows],
                        msend_sems.at[e, hop],
                        mrecv_sems.at[me],
                        2 * there + e,
                    ),
                )
                for e, s in enumerate((tkeys, tvals))
            ] + [
                (
                    e,
                    remote(
                        s.at[:, pl.ds(pl.multiple_of(base + e * local, 128), step_off)],
                        d.at[mine_rows],
                        tsend_sems.at[kind, e, hop],
                        trecv_sems.at[kind, me],
                        2 * there + e,
                    ),
                )
                for kind, (s, d) in enumerate(((tkeys, tk), (tvals, tv)))
                for e in range(2)
            ]
            for e, c in copies:
                if hop > 0:
                    c.start()
                else:
                    pl.when(core != e)(c.start)
                text.append((e, hop, c))

    def text_arrived(kind):
        own_text[kind].wait()
        d = (tk, tv)[kind]
        for k in range(1, n):
            src = lax.rem(me + k, n)
            block = d.at[pl.ds(src * trows, trows)]
            remote(
                block, block, tsend_sems.at[0, 0, 0], trecv_sems.at[kind, src], sibling
            ).wait_recv()

    def middle_arrived():
        own_middle(0).wait()
        for k in range(1, n):
            src = lax.rem(me + k, n)
            block = tmid.at[core, pl.ds(src * trows, trows)]
            remote(block, block, msend_sems.at[0, 0], mrecv_sems.at[src], sibling).wait_recv()

    def middle(kind):
        return remote(
            tmid.at[kind], tmid.at[kind], msib_sems.at[0], msib_sems.at[1], sibling
        )

    def prepare():
        own_table.wait()
        picks = (
            lax.broadcasted_iota(jnp.int32, (table.shape[1], n), 0) == levels[...]
        ).astype(jnp.float32)
        picks = jnp.transpose(picks).astype(jnp.bfloat16)
        drift, gain, gate = (
            jnp.dot(picks, table[kind], preferred_element_type=jnp.float32) for kind in range(3)
        )
        full[rows:, :] = drift.astype(jnp.bfloat16)
        mods[0] = 1.0 + gain
        mods[1] = gate

    fresh_row = lax.broadcasted_iota(jnp.int32, (2 * span, 1024), 0) >= span

    def rows_in(chip, opening):
        at = pl.ds(pl.multiple_of(chip * 2 * span, 2 * span), 2 * span)
        fresh = fresh_row & (chip == n // 2 - 1)
        later = lax.rem(2 * chip + 2, n)
        total = jnp.zeros((2 * span, 128), jnp.float32)
        for c in range(0, width, 1024):
            block = slice(c, c + 1024)
            new = incoming[0, :, block].astype(jnp.float32)
            x = jnp.concatenate(
                [
                    first[2 * chip, :, block].astype(jnp.float32),
                    first[2 * chip + 1, :, block].astype(jnp.float32),
                ],
                axis=0,
            )
            x = jnp.where(fresh, jnp.concatenate([new, new], axis=0), x)
            gain = jnp.concatenate(
                [
                    jnp.broadcast_to(mods[0, pl.ds(s, 1), block], (span, 1024))
                    for s in (2 * chip + 1, later)
                ],
                axis=0,
            )
            full[at, block] = (x * gain).astype(jnp.bfloat16)
            y = x * x
            for e in range(0, 1024, 128):
                total = total + y[:, e : e + 128]
        squares[at, :] = total

    def columns_in(step, source):
        fresh_from = rows - span

        def on_chip(chip, opening):
            at = pl.ds(pl.multiple_of(chip * pair, 128), pair)
            unpack(source, chip, piece_f32)
            piece_f32[fresh_from:, :] = incoming[step, :, at].astype(jnp.float32)
            x = piece_f32[...]
            piece_bf16[...] = (x * spread(mods.at[0], at)).astype(jnp.bfloat16)
            y = x * x
            total = y[:, :128]
            for e in range(128, pair, 128):
                total = total + y[:, e : e + 128]
            part = dot_nt(piece_bf16[...], wqkv[:, at])
            squares[...] = total if opening else squares[...] + total
            acc[...] = part if opening else acc[...] + part

        return on_chip

    def features_in(source):
        def on_chip(chip, opening):
            at = pl.ds(pl.multiple_of(chip * pair, 128), pair)
            unpack(source, chip, piece_bf16)
            part = dot_nt(piece_bf16[...], wo[:, at])
            oacc[...] = part if opening else oacc[...] + part

        return on_chip

    part = width // FIRST_CHUNKS
    cuts = (0, rows, blocks)

    def block_view(phase):
        return lambda slot, ch: gathered.at[phase, slot, pl.ds(cuts[ch], cuts[ch + 1] - cuts[ch])]

    own_at = pl.ds(start_col, local)
    start, run, finish = gather(
        lambda slot, ch: first.at[slot, :, pl.ds(ch * part, part)], FIRST_CHUNKS, 0
    )
    start(range(FIRST_CHUNKS))
    prepare()
    run(rows_in, lambda: send_text([2, 4, 6, 1, 3, 5, 7, 0]))
    for step in range(STEPS):
        if step == 0:
            for item in loads[:2]:
                item.wait()
            result = dot_nt(full[...], wqkv[: 2 * local])
            acc[:, : 2 * local] = result[:rows]
            shifted[:, : 2 * local] = result[rows:]
        r = lax.rsqrt(
            jnp.sum(squares[...], axis=-1, keepdims=True) * (1.0 / width) + 1e-06
        )

        def projected_by(j):
            at = pl.ds(j * local, local)
            return r * acc[:, at] + spread(shifted, at)

        q = projected_by(0)
        ssend[step, 0:1] = dot_nt(ones, q * q)[0:1]
        k_ = projected_by(1)
        ssend[step, 1:2] = dot_nt(ones, k_ * k_)[0:1]
        for k in range(1, n):
            c = remote(
                ssend.at[step],
                srecv.at[step, me],
                ssend_sems.at[step, k],
                srecv_sems.at[step, me],
                lax.rem(me + k, n),
            )
            c.start()
            pending.append(c)
        qb[...] = (q * qg).astype(jnp.bfloat16)
        kb[...] = (k_ * kg).astype(jnp.bfloat16)
        xsend[step, 0] = qb[:, pl.ds(mid, shared)]
        xsend[step, 1] = kb[:, pl.ds(mid, shared)]
        swap = remote(
            xsend.at[step], xrecv.at[step], xsend_sems.at[step], xrecv_sems.at[step], sibling
        )
        swap.start()
        srecv[step, me] = ssend[step]
        if step == 0:
            loads[2].wait()
            result = dot_nt(full[...], wqkv[2 * local :])
            acc[:, 2 * local :] = result[:rows]
            shifted[:, 2 * local :] = result[rows:]
            for s in range(n - 1):
                own_cols[s * span : (s + 1) * span, :] = first[s, :, own_at].astype(jnp.float32)
        own_cols[rows - span :, :] = incoming[step, :, own_at].astype(jnp.float32)
        vb[...] = projected_by(2).astype(jnp.bfloat16)
        for i in range(full_heads):
            raw_self[i] = dot_nt(qb[:, head_at(i)], kb[:, head_at(i)])
            if step > 0:
                raw_text[i] = dot_nt(qb[:, head_at(i)], tk[:, i * head : (i + 1) * head])
        swap.wait()
        qb[:, pl.ds(mid, shared)] = qb[:, pl.ds(mid, shared)] + xrecv[step, 0]
        kb[:, pl.ds(mid, shared)] = kb[:, pl.ds(mid, shared)] + xrecv[step, 1]
        raw_self[full_heads] = dot_nt(qb[:, head_at(full_heads)], kb[:, head_at(full_heads)])
        if step > 0:
            raw_text[full_heads] = dot_nt(qb[:, head_at(full_heads)], tmid[0])
        for k in range(1, n):
            src = lax.rem(me + k, n)
            remote(
                ssend.at[step],
                srecv.at[step, src],
                ssend_sems.at[step, k],
                srecv_sems.at[step, src],
                sibling,
            ).wait_recv()
        total = jnp.sum(srecv[step], axis=0)
        inv = lax.rsqrt(total * (1.0 / width) + 1e-06)
        q_col = jnp.transpose(jnp.broadcast_to(inv[0:1], (rows, rows)))[:, 0:1] * scale
        k_row = inv[1:2]

        def self_part(i):
            s = raw_self[i] * q_col * k_row
            s = jnp.where(allowed, s, -1e30)
            w = jnp.exp(s - jnp.max(s, axis=-1, keepdims=True))
            return jnp.dot(
                w.astype(jnp.bfloat16), vb[:, head_at(i)], preferred_element_type=jnp.float32
            ) / jnp.sum(w, axis=-1, keepdims=True)

        def text_part(i, values):
            t = raw_text[i] * q_col
            w = jnp.exp(t - jnp.max(t, axis=-1, keepdims=True))
            return jnp.dot(
                w.astype(jnp.bfloat16), values, preferred_element_type=jnp.float32
            ) / jnp.sum(w, axis=-1, keepdims=True)

        if step == 0:
            for i in range(full_heads + 1):
                placed[:, i * head : (i + 1) * head] = self_part(i)
            middle_arrived()
            for kind in range(2):
                pl.when(core == kind)(middle(kind).start)
            text_arrived(0)
            for i in range(full_heads):
                raw_text[i] = dot_nt(qb[:, head_at(i)], tk[:, i * head : (i + 1) * head])
            text_arrived(1)
            loads[3].wait()
        mine_block = gathered.at[2 * step, me]
        start, run, finish_next = gather(block_view(2 * step), CHUNKS, 2 * step + 1)
        for i in range(full_heads + 1):
            if step == 0 and i == full_heads:
                middle(1 - core).wait_recv()
                raw_text[i] = dot_nt(qb[:, head_at(i)], tmid[0])
            values = tv[:, i * head : (i + 1) * head] if i < full_heads else tmid[1]
            both = placed[:, i * head : (i + 1) * head] if step == 0 else self_part(i)
            pack(both + text_part(i, values), i, mine_block)
            if i == 0:
                start([0])
        start([1])
        finish()
        finish = finish_next
        run(features_in(gathered.at[2 * step]))
        state = jnp.where(
            mine, own_cols[...] + spread(mods.at[1], own_at) * oacc[...], 0.0
        )
        state = jnp.concatenate([state[rows - span :], state[: rows - span]], axis=0)
        if step < STEPS - 1:
            placed[...] = state
            start, run, finish_next = gather(block_view(2 * step + 1), CHUNKS, 2 * step + 2)
            for i in range(full_heads + 1):
                pack(placed[:, head_at(i)], i, gathered.at[2 * step + 1, me])
                if i == 0:
                    start([0])
            start([1])
            finish()
            finish = finish_next
            own_cols[...] = state.astype(jnp.bfloat16).astype(jnp.float32)
            run(columns_in(step + 1, gathered.at[2 * step + 1]))
        else:
            osend[...] = state.reshape(n, span, local).astype(jnp.bfloat16)
            for k in range(1, n):
                target = lax.rem(me + k, n)
                c = remote(
                    osend.at[target],
                    orecv.at[me],
                    osend_sems.at[k],
                    orecv_sems.at[me],
                    target,
                )
                c.start()
                pending.append(c)
            orecv[me] = osend[me]
    for k in range(1, n):
        src = lax.rem(me + k, n)
        remote(
            osend.at[src], orecv.at[src], osend_sems.at[k], orecv_sems.at[src], sibling
        ).wait_recv()
    assemble(orecv, out, 0, span)
    for e, hop, c in text:
        if hop > 0:
            c.wait_send()
        else:
            pl.when(core != e)(c.wait_send)
    middle(core).wait_send()
    finish()
    for c in pending:
        c.wait_send()


def per_device_fused(
    hidden,
    incoming,
    levels,
    mod_table,
    query_weight,
    key_weight,
    value_weight,
    output_weight,
    query_gain,
    key_gain,
    text_keys,
    text_values,
):
    n = lax.axis_size("queue")
    span, width = hidden.shape
    cols = query_weight.shape[1]
    head = width // HEADS
    local = -(-cols // head) * head
    shared = 2 * local - 2 * cols
    step_off = 2 * cols - local
    pair = 2 * cols
    rows = n * span
    text = n * text_keys.shape[0]
    vmem = pl.BlockSpec(memory_space=pltpu.VMEM)
    anywhere = pl.BlockSpec(memory_space=pl.ANY)
    dma = pltpu.SemaphoreType.DMA
    bf16, f32 = jnp.bfloat16, jnp.float32
    most = max(FIRST_CHUNKS, CHUNKS)
    return pl.pallas_call(
        functools.partial(fused_kernel, n, cols),
        out_shape=jax.ShapeDtypeStruct((span, width), hidden.dtype),
        in_specs=[anywhere, vmem, vmem] + [anywhere] * 5 + [vmem] * 2 + [anywhere] * 2,
        out_specs=vmem,
        scratch_shapes=[
            pltpu.VMEM((3, mod_table.shape[0], width), bf16),
            pltpu.VMEM((2, n, width), f32),
            pltpu.VMEM((3 * local, width), bf16),
            pltpu.VMEM((local, width), bf16),
            pltpu.VMEM((n, span, width), bf16),
            pltpu.VMEM((2 * STEPS - 1, n, rows * cols // head, head), bf16),
            pltpu.VMEM((rows + n, width), bf16),
            pltpu.VMEM((rows, 3 * local), f32),
            pltpu.VMEM((n, 3 * local), f32),
            pltpu.VMEM((rows, 128), f32),
            pltpu.VMEM((rows, pair), f32),
            pltpu.VMEM((rows, pair), bf16),
            pltpu.VMEM((rows, local), f32),
            pltpu.VMEM((rows, local), f32),
            pltpu.VMEM((rows, local), f32),
            pltpu.VMEM((rows, local), bf16),
            pltpu.VMEM((rows, local), bf16),
            pltpu.VMEM((rows, local), bf16),
            pltpu.VMEM((local // head, rows, rows), f32),
            pltpu.VMEM((local // head, rows, text), f32),
            pltpu.VMEM((STEPS, 2, rows, shared), bf16),
            pltpu.VMEM((STEPS, 2, rows, shared), bf16),
            pltpu.VMEM((STEPS, 2, rows), f32),
            pltpu.VMEM((STEPS, n, 2, rows), f32),
            pltpu.VMEM((text, step_off), bf16),
            pltpu.VMEM((text, step_off), bf16),
            pltpu.VMEM((2, text, shared), bf16),
            pltpu.VMEM((n, span, local), bf16),
            pltpu.VMEM((n, span, local), bf16),
            dma((9,)),
            dma((2, 15, most)),
            dma((2 * STEPS, n, most)),
            dma((STEPS, n)),
            dma((STEPS, n)),
            dma((STEPS,)),
            dma((STEPS,)),
            dma((2, 2, n // 2)),
            dma((2, n)),
            dma((2, n // 2)),
            dma((n,)),
            dma((2,)),
            dma((n,)),
            dma((n,)),
        ],
        compiler_params=pltpu.CompilerParams(
            collective_id=0, has_side_effects=True, vmem_limit_bytes=60 * 1024 * 1024
        ),
    )(
        hidden,
        incoming,
        levels.reshape(1, n),
        mod_table.transpose(1, 0, 2),
        query_weight.T,
        key_weight.T,
        value_weight.T,
        output_weight.T,
        query_gain.reshape(1, width),
        key_gain.reshape(1, width),
        text_keys,
        text_values,
    )


def fits_fused(count, rows_total, width, groups):
    head = width // HEADS
    cols = width // count
    span = rows_total // (count * groups)
    return (
        count // 4 == 4
        and count % 4 == 0
        and width % 1024 == 0
        and head == 128
        and span == 8
        and (2 * cols) % head == 0
        and cols % head == head // 2
        and cols > head
        and count * span == 128
    )


def choose(mesh):
    def run(hidden, incoming, levels, mod_table, *rest):
        count = lax.axis_size("queue")
        if fits_fused(count, hidden.shape[0] * count, hidden.shape[1], 1):
            return per_device_fused(hidden, incoming, levels, mod_table, *rest)
        return per_device(hidden, incoming, levels, mod_table, *rest)

    return run


def solution(mesh):
    in_specs = (
        P(("groups", "queue"), None),
        P(None, "groups", None),
        P(),
        P(),
        P(None, "queue"),
        P(None, "queue"),
        P(None, "queue"),
        P(None, "queue"),
        P(),
        P(),
        P(("groups", "queue"), None),
        P(("groups", "queue"), None),
    )
    out_specs = P(("groups", "queue"), None)
    return jax.shard_map(
        choose(mesh), mesh=mesh, in_specs=in_specs, out_specs=out_specs, check_vma=False
    )
```

```python
import functools
import math

import jax
import jax.numpy as jnp
from jax import lax
from jax.experimental import pallas as pl
from jax.experimental.pallas import tpu as pltpu
from jax.sharding import PartitionSpec as P

HEADS = 40
STEPS = 2
FIRST_CHUNKS = 2
CHUNKS = 2
HALVES_ORDER = (
    "l10", "s00", "a00", "l20", "a10", "l30", "s10", "b00",
    "l11", "s01", "a20", "l21", "a01", "s20", "a30", "l31",
    "b10", "s30", "a11", "s11", "b20", "b30", "h00", "b01",
    "s21", "a21", "s31", "a31", "b11", "b21", "b31", "h01",
)


def passed_along(value, axis, steps):
    count = lax.axis_size(axis)
    initial, last = (max(0, -steps), min(count, count - steps))
    return lax.ppermute(value, axis, [(source, source + steps) for source in range(initial, last)])


def normalize(values):
    return values * lax.rsqrt(jnp.mean(values * values, axis=-1, keepdims=True) + 1e-06)


def softmax_rounded(scores):
    row_max = jnp.max(scores, axis=-1, keepdims=True)
    weights = jnp.exp(scores - row_max)
    return (weights / jnp.sum(weights, axis=-1, keepdims=True)).astype(jnp.bfloat16)


def pad_slots(values, slot_total):
    missing = slot_total - values.shape[1]
    filler = jnp.zeros((values.shape[0], missing, values.shape[2]), values.dtype)
    return jnp.concatenate([values, filler], axis=1)


def causal_block(queries, keys_all, values_all, span_rows, score_scale):
    total_rows = queries.shape[0]
    block_rows = min(512, total_rows)
    scores = (
        jnp.einsum("qsd,ksd->sqk", queries, keys_all, preferred_element_type=jnp.float32)
        * score_scale
    )
    allowed = (
        jnp.arange(0, block_rows)[:, None] // span_rows
        >= jnp.arange(block_rows)[None, :] // span_rows
    )
    scores = jnp.where(allowed[None], scores, -1e30)
    result = jnp.einsum(
        "sqk,ksd->qsd", softmax_rounded(scores), values_all, preferred_element_type=jnp.float32
    )
    pieces = result.astype(jnp.bfloat16)
    return pieces


def text_attend(queries, text_k, text_v, score_scale):
    scores = (
        jnp.einsum("qsd,tsd->sqt", queries, text_k, preferred_element_type=jnp.float32)
        * score_scale
    )
    return jnp.einsum(
        "sqt,tsd->qsd", softmax_rounded(scores), text_v, preferred_element_type=jnp.float32
    ).astype(jnp.bfloat16)


def per_device(
    hidden,
    incoming,
    levels,
    mod_table,
    query_weight,
    key_weight,
    value_weight,
    output_weight,
    query_gain,
    key_gain,
    text_keys,
    text_values,
):
    own_index = lax.axis_index("queue")
    queue_size = lax.axis_size("queue")
    span_rows, model_width = hidden.shape
    head_size = model_width // HEADS
    score_scale = 1.0 / math.sqrt(head_size)
    slot_total = -(-HEADS // queue_size) * queue_size
    own_level = lax.dynamic_index_in_dim(levels, own_index, 0, keepdims=False)
    modulation = lax.dynamic_index_in_dim(mod_table, own_level, 0, keepdims=False).astype(
        jnp.float32
    )
    stacked_weights = jnp.stack([query_weight, key_weight, value_weight])
    text_local = text_keys.shape[0]
    text_k_slots, text_v_slots = (
        lax.all_to_all(
            pad_slots(text_keys.reshape(text_local, HEADS, head_size), slot_total),
            "queue",
            split_axis=1,
            concat_axis=0,
            tiled=True,
        ),
        lax.all_to_all(
            pad_slots(text_values.reshape(text_local, HEADS, head_size), slot_total),
            "queue",
            split_axis=1,
            concat_axis=0,
            tiled=True,
        ),
    )
    queue_state = hidden
    for section_index in range(STEPS):
        shifted = passed_along(queue_state, "queue", 1)
        queue_state = jnp.where(own_index == 0, incoming[section_index], shifted)
        current = queue_state.astype(jnp.float32)
        modulated = (normalize(current) * (1.0 + modulation[1]) + modulation[0]).astype(
            jnp.bfloat16
        )
        columns = jnp.einsum(
            "rd,cdw->crw",
            lax.all_gather(modulated, "queue", axis=0, tiled=True),
            stacked_weights,
            preferred_element_type=jnp.float32,
        )
        own_rows = lax.all_to_all(
            columns.astype(jnp.bfloat16), "queue", split_axis=1, concat_axis=2, tiled=True
        ).astype(columns.dtype)
        query_heads = (
            (normalize(own_rows[0]) * query_gain)
            .astype(jnp.bfloat16)
            .reshape(span_rows, HEADS, head_size)
        )
        key_heads = (
            (normalize(own_rows[1]) * key_gain)
            .astype(jnp.bfloat16)
            .reshape(span_rows, HEADS, head_size)
        )
        value_heads = own_rows[2].astype(jnp.bfloat16).reshape(span_rows, HEADS, head_size)
        query_slots, key_slots, value_slots = (
            lax.all_to_all(
                pad_slots(query_heads, slot_total), "queue", split_axis=1, concat_axis=0, tiled=True
            ),
            lax.all_to_all(
                pad_slots(key_heads, slot_total), "queue", split_axis=1, concat_axis=0, tiled=True
            ),
            lax.all_to_all(
                pad_slots(value_heads, slot_total), "queue", split_axis=1, concat_axis=0, tiled=True
            ),
        )
        attended_slots = causal_block(query_slots, key_slots, value_slots, span_rows, score_scale)
        crossed_slots = text_attend(query_slots, text_k_slots, text_v_slots, score_scale)
        attended_back, crossed_back = (
            lax.all_to_all(attended_slots, "queue", split_axis=0, concat_axis=1, tiled=True),
            lax.all_to_all(crossed_slots, "queue", split_axis=0, concat_axis=1, tiled=True),
        )
        attended = attended_back[:, :HEADS]
        crossed = crossed_back[:, :HEADS]
        combined = (
            (attended.astype(jnp.float32) + crossed.astype(jnp.float32))
            .astype(jnp.bfloat16)
            .reshape(span_rows, model_width)
        )
        out_columns = jnp.dot(
            lax.all_gather(combined, "queue", axis=0, tiled=True),
            output_weight,
            preferred_element_type=jnp.float32,
        )
        projected = lax.all_to_all(
            out_columns.astype(jnp.bfloat16), "queue", split_axis=0, concat_axis=1, tiled=True
        ).astype(out_columns.dtype)
        queue_state = (current + modulation[2] * projected).astype(jnp.bfloat16)
    return queue_state


def dot_nt(a, b):
    return lax.dot_general(a, b, (((1,), (1,)), ((), ())), preferred_element_type=jnp.float32)


def fused_kernel(
    n,
    cols,
    hidden,
    incoming,
    levels,
    table_hbm,
    wq_hbm,
    wk_hbm,
    wv_hbm,
    wo_hbm,
    q_gain,
    k_gain,
    tkeys,
    tvals,
    out,
    table,
    mods,
    wqkv,
    wo,
    first,
    gathered,
    full,
    acc,
    shifted,
    squares,
    piece_f32,
    piece_bf16,
    oacc,
    own_cols,
    placed,
    qb,
    kb,
    vb,
    raw_self,
    raw_text,
    xsend,
    xrecv,
    ssend,
    srecv,
    tk,
    tv,
    tmid,
    osend,
    orecv,
    load_sems,
    gsend_sems,
    grecv_sems,
    ssend_sems,
    srecv_sems,
    xsend_sems,
    xrecv_sems,
    tsend_sems,
    trecv_sems,
    msend_sems,
    mrecv_sems,
    msib_sems,
    osend_sems,
    orecv_sems,
):
    me = lax.axis_index("queue")
    span, width = hidden.shape
    head = width // HEADS
    rows = n * span
    pair = 2 * cols
    local = placed.shape[1]
    blocks = gathered.shape[2]
    shared = 2 * local - pair
    step_off = pair - local
    pad = local - cols
    core = lax.rem(me, 2)
    row = lax.rem(me // 2, 2)
    depth = me // 4
    sibling = me + 1 - 2 * core
    start_col = pl.multiple_of((me // 2) * pair + core * step_off, 128)
    mid = pl.multiple_of((1 - core) * step_off, 128)
    mid_start = pl.multiple_of((me // 2) * pair + step_off, 128)
    own_start = pl.multiple_of((me // 2) * pair + core * local, 128)
    trows = tkeys.shape[0]
    scale = 1.0 / math.sqrt(head)

    upper = depth // 2
    folded_depth = depth + upper * (3 - 2 * depth)

    def nth(k):
        x = (folded_depth, 1 - folded_depth, 2, 3)[k]
        return x + upper * (3 - 2 * x)

    along = [4 * nth(k) + 2 * row + core for k in range(4)]
    beside = [4 * nth(k) + 2 * (1 - row) + core for k in range(4)]
    across = me + 2 - 4 * row

    def flip(slot):
        return slot + 1 - 2 * core

    barrier = pltpu.get_barrier_semaphore()
    for k in range(1, n):
        pl.semaphore_signal(
            barrier,
            inc=1,
            device_id={"queue": lax.rem(me + k, n)},
            device_id_type=pl.DeviceIdType.MESH,
        )
    own = pltpu.make_async_copy(hidden, first.at[me], load_sems.at[4])
    own.start()
    own_table = pltpu.make_async_copy(table_hbm, table, load_sems.at[7])
    own_table.start()
    blank = jnp.zeros((pad, width), jnp.bfloat16)
    gap = (1 - core) * cols
    for j in range(3):
        wqkv[pl.ds(pl.multiple_of(j * local + gap, pad), pad), :] = blank
    wo[pl.ds(pl.multiple_of(gap, pad), pad), :] = blank
    loads = [
        pltpu.make_async_copy(
            s, wqkv.at[pl.ds(pl.multiple_of(j * local + core * pad, pad), cols)], load_sems.at[j]
        )
        for j, s in enumerate((wq_hbm, wk_hbm, wv_hbm))
    ]
    loads.append(
        pltpu.make_async_copy(
            wo_hbm, wo.at[pl.ds(pl.multiple_of(core * pad, pad), cols)], load_sems.at[3]
        )
    )
    own_text = [
        pltpu.make_async_copy(
            s.at[:, pl.ds(own_start, step_off)], d.at[pl.ds(me * trows, trows)], load_sems.at[5 + i]
        )
        for i, (s, d) in enumerate(((tkeys, tk), (tvals, tv)))
    ]

    def own_middle(kind):
        return pltpu.make_async_copy(
            (tkeys, tvals)[kind].at[:, pl.ds(mid_start, shared)],
            tmid.at[kind, pl.ds(me * trows, trows)],
            load_sems.at[8],
        )

    for kind in range(2):

        @pl.when(core == kind)
        def _():
            own_middle(kind).start()

    for item in loads + own_text:
        item.start()
    own.wait()
    pl.semaphore_wait(barrier, n - 1)

    pending = []

    def remote(src, dst, send, recv, target):
        return pltpu.make_async_remote_copy(
            src_ref=src,
            dst_ref=dst,
            send_sem=send,
            recv_sem=recv,
            device_id={"queue": target},
            device_id_type=pl.DeviceIdType.MESH,
        )

    finishes = []

    def gather(view, chunks, phase):
        def copy(slot, ch, kind, target):
            return remote(
                view(slot, ch),
                view(slot, ch),
                gsend_sems.at[phase, kind, ch],
                grecv_sems.at[phase, slot, ch],
                target,
            )

        def push(slot, ch, kind, target):
            c = copy(slot, ch, kind, target)
            c.start()
            finishes.append(c)

        def arrived(slot, ch):
            copy(slot, ch, 0, sibling).wait_recv()

        def start(some):
            for ch in some:
                push(me, ch, 0, across)
            for k in range(1, 4):
                for ch in some:
                    push(me, ch, k, along[k])
            for ch in some:
                push(me, ch, 4, sibling)

        def line(k, some):
            for ch in some:
                arrived(along[k], ch)
                push(along[k], ch, 4 + k, across)
                push(along[k], ch, 7 + k, sibling)

        def side(k, some):
            for ch in some:
                arrived(beside[k], ch)
                push(beside[k], ch, 11 + k, sibling)

        def run_rows(on_chip, late):
            every = range(chunks)

            def chip(slot):
                for ch in every:
                    arrived(flip(slot), ch)
                on_chip(slot // 2)

            line(1, every)
            chip(me)
            side(0, every)
            chip(along[1])
            line(2, every)
            chip(beside[0])
            side(1, every)
            chip(along[2])
            line(3, every)
            late()
            chip(beside[1])
            side(2, every)
            chip(along[3])
            side(3, every)
            chip(beside[2])
            chip(beside[3])

        def run_halves(on_chip, hook):
            slots = {"a": along, "b": beside}
            opened = set()
            for event in HALVES_ORDER:
                what, k, half = event[0], int(event[1]), int(event[2])
                if what == "l":
                    line(k, [half])
                elif what == "s":
                    side(k, [half])
                elif what == "h":
                    hook(half)
                else:
                    slot = slots[what][k]
                    arrived(flip(slot), half)
                    on_chip(slot // 2, half, half not in opened)
                    opened.add(half)

        return start, run_rows, run_halves

    full_heads = step_off // head
    half_rows = rows // 2
    quarter = half_rows // 2
    half_blocks = blocks // 2
    low = lax.broadcasted_iota(jnp.int32, (quarter, shared), 1) < shared // 2
    owned = (
        lax.broadcasted_iota(jnp.int32, (half_rows, shared), 1) // (shared // 2)
    ) == core

    def head_at(i):
        if i == full_heads:
            return pl.ds(mid, head)
        return pl.ds(pl.multiple_of(core * shared + i * head, 128), head)

    def pack(value, i, half, dst):
        base = half * half_blocks + i * half_rows
        if i < full_heads:
            dst[base : base + half_rows, :] = value.astype(jnp.bfloat16)
        else:
            kept = jnp.where(owned, value, 0.0)
            dst[base : base + quarter, :] = (
                kept[:quarter] + pltpu.roll(kept[quarter:], shared // 2, 1)
            ).astype(jnp.bfloat16)

    def unpack(buf, chip, half, dst):
        a, b = buf.at[2 * chip], buf.at[2 * chip + 1]
        base = half * half_blocks
        for i in range(full_heads):
            part = slice(base + i * half_rows, base + (i + 1) * half_rows)
            dst[:, i * head : (i + 1) * head] = a[part, :].astype(dst.dtype)
            dst[:, local + i * head : local + (i + 1) * head] = b[part, :].astype(dst.dtype)
        base = base + full_heads * half_rows
        fa, fb = (r[base : base + quarter, :].astype(jnp.float32) for r in (a, b))
        dst[:quarter, step_off:local] = jnp.where(low, fa, fb).astype(dst.dtype)
        dst[quarter:, step_off:local] = pltpu.roll(
            jnp.where(low, fb, fa), shared // 2, 1
        ).astype(dst.dtype)

    lane = lax.broadcasted_iota(jnp.int32, (half_rows, local), 1)
    shift = core * pad
    mine = (lane >= shift) & (lane < shift + cols)

    def assemble(buf, dst, base, count):
        for p in range(n // 2):
            a = buf[2 * p, :count]
            b = buf[2 * p + 1, :count]
            at = p * pair
            kept = pl.ds(base, count)
            dst[kept, at : at + step_off] = a[:, :step_off].astype(dst.dtype)
            dst[kept, at + step_off : at + local] = (
                a[:, step_off:].astype(jnp.float32) + b[:, :shared].astype(jnp.float32)
            ).astype(dst.dtype)
            dst[kept, at + local : at + pair] = b[:, shared:].astype(dst.dtype)

    def span_of(block, step):
        return (block + n - STEPS + 1 + step) % n

    def spread(ref, at, step, half):
        first_block = half * n // 2
        return jnp.concatenate(
            [
                jnp.broadcast_to(
                    ref[span_of(i, step) : span_of(i, step) + 1, at], (span, at.size)
                )
                for i in range(first_block, first_block + n // 2)
            ],
            axis=0,
        )

    qg = q_gain[:, pl.ds(start_col, local)]
    kg = k_gain[:, pl.ds(start_col, local)]
    ones = jnp.ones((8, local), jnp.float32)
    def causal(step, half, keys):
        shape = (half_rows, keys)
        moved = half * n // 2 + n - STEPS + 1 + step
        at_row = lax.broadcasted_iota(jnp.int32, shape, 0) // span + moved
        at_col = lax.broadcasted_iota(jnp.int32, shape, 1) // span + n - STEPS + 1 + step
        return lax.rem(at_row, n) >= lax.rem(at_col, n)

    text = []

    def send_text(hops):
        for hop in hops:
            there = lax.rem(me // 2 + hop, n // 2)
            base = pl.multiple_of(there * pair, 128)
            mine_rows = pl.ds(me * trows, trows)
            copies = [
                (
                    e,
                    remote(
                        s.at[:, pl.ds(pl.multiple_of(base + step_off, 128), shared)],
                        tmid.at[e, mine_rows],
                        msend_sems.at[e, hop],
                        mrecv_sems.at[me],
                        2 * there + e,
                    ),
                )
                for e, s in enumerate((tkeys, tvals))
            ] + [
                (
                    e,
                    remote(
                        s.at[:, pl.ds(pl.multiple_of(base + e * local, 128), step_off)],
                        d.at[mine_rows],
                        tsend_sems.at[kind, e, hop],
                        trecv_sems.at[kind, me],
                        2 * there + e,
                    ),
                )
                for kind, (s, d) in enumerate(((tkeys, tk), (tvals, tv)))
                for e in range(2)
            ]
            for e, c in copies:
                if hop > 0:
                    c.start()
                else:
                    pl.when(core != e)(c.start)
                text.append((e, hop, c))

    def text_arrived(kind):
        own_text[kind].wait()
        d = (tk, tv)[kind]
        for k in range(1, n):
            src = lax.rem(me + k, n)
            block = d.at[pl.ds(src * trows, trows)]
            remote(
                block, block, tsend_sems.at[0, 0, 0], trecv_sems.at[kind, src], sibling
            ).wait_recv()

    def middle_arrived():
        own_middle(0).wait()
        for k in range(1, n):
            src = lax.rem(me + k, n)
            block = tmid.at[core, pl.ds(src * trows, trows)]
            remote(block, block, msend_sems.at[0, 0], mrecv_sems.at[src], sibling).wait_recv()

    def middle(kind):
        return remote(
            tmid.at[kind], tmid.at[kind], msib_sems.at[0], msib_sems.at[1], sibling
        )

    def prepare():
        own_table.wait()
        picks = (
            lax.broadcasted_iota(jnp.int32, (table.shape[1], n), 0) == levels[...]
        ).astype(jnp.float32)
        picks = jnp.transpose(picks).astype(jnp.bfloat16)
        drift, gain, gate = (
            jnp.dot(picks, table[kind], preferred_element_type=jnp.float32) for kind in range(3)
        )
        full[rows:, :] = drift.astype(jnp.bfloat16)
        mods[0] = 1.0 + gain
        mods[1] = gate

    fresh_row = lax.broadcasted_iota(jnp.int32, (2 * span, 1024), 0) >= span

    def rows_in(chip):
        place = lax.rem(chip + STEPS // 2, n // 2)
        at = pl.ds(pl.multiple_of(place * 2 * span, 2 * span), 2 * span)
        fresh = fresh_row & (chip == n // 2 - 1)
        later = lax.rem(2 * chip + 2, n)
        total = jnp.zeros((2 * span, 128), jnp.float32)
        for c in range(0, width, 1024):
            block = slice(c, c + 1024)
            new = incoming[0, :, block].astype(jnp.float32)
            x = jnp.concatenate(
                [
                    first[2 * chip, :, block].astype(jnp.float32),
                    first[2 * chip + 1, :, block].astype(jnp.float32),
                ],
                axis=0,
            )
            x = jnp.where(fresh, jnp.concatenate([new, new], axis=0), x)
            gain = jnp.concatenate(
                [
                    jnp.broadcast_to(mods[0, pl.ds(s, 1), block], (span, 1024))
                    for s in (2 * chip + 1, later)
                ],
                axis=0,
            )
            full[at, block] = (x * gain).astype(jnp.bfloat16)
            y = x * x
            for e in range(0, 1024, 128):
                total = total + y[:, e : e + 128]
        squares[at, :] = total

    def half_at(half):
        return pl.ds(half * half_rows, half_rows)

    def columns_in(step, source):
        def on_chip(chip, half, opening):
            at = pl.ds(pl.multiple_of(chip * pair, 128), pair)
            unpack(source, chip, half, piece_f32)
            if half == 0:
                piece_f32[:span, :] = incoming[step, :, at].astype(jnp.float32)
            x = piece_f32[...]
            piece_bf16[...] = (x * spread(mods.at[0], at, step, half)).astype(jnp.bfloat16)
            y = x * x
            total = y[:, :128]
            for e in range(128, pair, 128):
                total = total + y[:, e : e + 128]
            part = dot_nt(piece_bf16[...], wqkv[:, at])
            to = half_at(half)
            squares[to, :] = total if opening else squares[to, :] + total
            acc[to, :] = part if opening else acc[to, :] + part

        return on_chip

    def features_in(source):
        def on_chip(chip, half, opening):
            at = pl.ds(pl.multiple_of(chip * pair, 128), pair)
            unpack(source, chip, half, piece_bf16)
            part = dot_nt(piece_bf16[...], wo[:, at])
            to = half_at(half)
            oacc[to, :] = part if opening else oacc[to, :] + part

        return on_chip

    part = width // FIRST_CHUNKS

    def block_view(phase):
        return lambda slot, ch: gathered.at[phase, slot, pl.ds(ch * half_blocks, half_blocks)]

    own_at = pl.ds(start_col, local)

    def norm_copy(turn, k, src, target):
        return remote(
            ssend.at[turn],
            srecv.at[turn, src],
            ssend_sems.at[turn, k],
            srecv_sems.at[turn, src],
            target,
        )

    def swap_copy(turn):
        return remote(
            xsend.at[turn], xrecv.at[turn], xsend_sems.at[turn], xrecv_sems.at[turn], sibling
        )

    def projected_by(j, step, half):
        at = pl.ds(j * local, local)
        to = half_at(half)
        r = lax.rsqrt(
            jnp.sum(squares[to, :], axis=-1, keepdims=True) * (1.0 / width) + 1e-06
        )
        return r * acc[to, at] + spread(shifted, at, step, half)

    def square_sums(value):
        sums = dot_nt(ones, value * value)[0:1]
        return jnp.concatenate([sums, sums], axis=1)

    def launch(step, half):
        turn = 2 * step + half
        to = half_at(half)
        q = projected_by(0, step, half)
        ssend[turn, 0:1] = square_sums(q)
        k_ = projected_by(1, step, half)
        ssend[turn, 1:2] = square_sums(k_)
        for k in range(1, n):
            c = norm_copy(turn, k, me, lax.rem(me + k, n))
            c.start()
            pending.append(c)
        qb[to, :] = (q * qg).astype(jnp.bfloat16)
        kb[to, :] = (k_ * kg).astype(jnp.bfloat16)
        xsend[turn, 0] = qb[to, pl.ds(mid, shared)]
        xsend[turn, 1] = kb[to, pl.ds(mid, shared)]
        swap_copy(turn).start()
        srecv[turn, me] = ssend[turn]

    def swapped(turn, half):
        to = half_at(half)
        swap_copy(turn).wait()
        qb[to, pl.ds(mid, shared)] = qb[to, pl.ds(mid, shared)] + xrecv[turn, 0]
        kb[to, pl.ds(mid, shared)] = kb[to, pl.ds(mid, shared)] + xrecv[turn, 1]

    k_rows = {}

    def norms_arrived(turn):
        for k in range(1, n):
            norm_copy(turn, k, lax.rem(me + k, n), sibling).wait_recv()
        inv = lax.rsqrt(jnp.sum(srecv[turn], axis=0) * (1.0 / width) + 1e-06)
        k_rows[turn] = inv[1:2]
        turned = jnp.transpose(jnp.broadcast_to(inv[0:1], (rows, rows)))
        return turned[:half_rows, 0:1] * scale

    def keys_of(step, half):
        return rows if step == 0 or half == 1 else half_rows

    def score_self(i, step, half):
        keys = keys_of(step, half)
        to = half_at(half)
        raw_self[i, to, :keys] = dot_nt(qb[to, head_at(i)], kb[:keys, head_at(i)])

    def score_text(i, half):
        keys = tk[:, i * head : (i + 1) * head] if i < full_heads else tmid[0]
        to = half_at(half)
        raw_text[i, to, :] = dot_nt(qb[to, head_at(i)], keys)

    low_keys = lax.broadcasted_iota(jnp.int32, (1, rows), 1) < half_rows

    def self_part(i, step, half, q_col):
        keys = keys_of(step, half)
        if keys == rows:
            k_row = jnp.where(low_keys, k_rows[2 * step], k_rows[2 * step + 1])
        else:
            k_row = k_rows[2 * step][:, :keys]
        s = raw_self[i, half_at(half), :keys] * q_col * k_row
        s = jnp.where(causal(step, half, keys), s, -1e30)
        w = jnp.exp(s - jnp.max(s, axis=-1, keepdims=True))
        return jnp.dot(
            w.astype(jnp.bfloat16), vb[:keys, head_at(i)], preferred_element_type=jnp.float32
        ) / jnp.sum(w, axis=-1, keepdims=True)

    def text_part(i, half, q_col):
        values = tv[:, i * head : (i + 1) * head] if i < full_heads else tmid[1]
        t = raw_text[i, half_at(half), :] * q_col
        w = jnp.exp(t - jnp.max(t, axis=-1, keepdims=True))
        return jnp.dot(
            w.astype(jnp.bfloat16), values, preferred_element_type=jnp.float32
        ) / jnp.sum(w, axis=-1, keepdims=True)

    def state_of(step, half):
        to = half_at(half)
        gate = spread(mods.at[1], own_at, step, half)
        return jnp.where(mine, own_cols[to, :] + gate * oacc[to, :], 0.0)

    def final_copy(src, dst, target):
        return remote(
            osend.at[src], orecv.at[dst], osend_sems.at[src], orecv_sems.at[dst], target
        )

    every_head = range(full_heads + 1)
    start, run_rows, _ = gather(
        lambda slot, ch: first.at[slot, :, pl.ds(ch * part, part)], FIRST_CHUNKS, 0
    )
    start(range(FIRST_CHUNKS))
    prepare()
    run_rows(rows_in, lambda: send_text([2, 4, 6, 1, 3, 5, 7, 0]))
    for item in loads[:2]:
        item.wait()
    result = dot_nt(full[...], wqkv[: 2 * local])
    acc[:, : 2 * local] = result[:rows]
    shifted[:, : 2 * local] = result[rows:]
    for half in range(2):
        launch(0, half)
    loads[2].wait()
    result = dot_nt(full[...], wqkv[2 * local :])
    acc[:, 2 * local :] = result[:rows]
    shifted[:, 2 * local :] = result[rows:]
    for i in range(n):
        rows_of = slice(i * span, (i + 1) * span)
        if i == STEPS - 1:
            own_cols[rows_of, :] = incoming[0, :, own_at].astype(jnp.float32)
        else:
            own_cols[rows_of, :] = first[(i - STEPS) % n, :, own_at].astype(jnp.float32)
    for half in range(2):
        vb[half_at(half), :] = projected_by(2, 0, half).astype(jnp.bfloat16)
        swapped(half, half)
    for half in range(2):
        for i in every_head:
            score_self(i, 0, half)
    q_cols = [norms_arrived(half) for half in range(2)]
    for half in range(2):
        for i in every_head:
            placed[half_at(half), i * head : (i + 1) * head] = self_part(i, 0, half, q_cols[half])
    middle_arrived()
    for kind in range(2):
        pl.when(core == kind)(middle(kind).start)
    text_arrived(0)
    for half in range(2):
        for i in range(full_heads):
            score_text(i, half)
    text_arrived(1)
    loads[3].wait()
    middle(1 - core).wait_recv()
    start, _, run_halves = gather(block_view(0), CHUNKS, 1)
    for half in range(2):
        score_text(full_heads, half)
        for i in every_head:
            both = placed[half_at(half), i * head : (i + 1) * head] + text_part(
                i, half, q_cols[half]
            )
            pack(both, i, half, gathered.at[0, me])
        start([half])

    for step in range(STEPS):
        last = step == STEPS - 1
        if not last:
            start_next, _, run_next = gather(block_view(2 * step + 1), CHUNKS, 2 * step + 2)

        def features_done(half):
            state = state_of(step, half)
            if last:
                spans = slice(half * n // 2, (half + 1) * n // 2)
                osend[spans] = state.reshape(n // 2, span, local).astype(jnp.bfloat16)
                for target in range(half * n // 2, (half + 1) * n // 2):
                    pl.when(me != target)(final_copy(target, me, target).start)
                return
            placed[half_at(half), :] = state
            for i in every_head:
                pack(placed[half_at(half), head_at(i)], i, half, gathered.at[2 * step + 1, me])
            start_next([half])
            own_cols[half_at(half), :] = state.astype(jnp.bfloat16).astype(jnp.float32)
            if half == 0:
                fresh = slice((STEPS - 2 - step) * span, (STEPS - 1 - step) * span)
                own_cols[fresh, :] = incoming[step + 1, :, own_at].astype(jnp.float32)

        run_halves(features_in(gathered.at[2 * step]), features_done)
        if last:
            break

        def columns_done(half):
            launch(step + 1, half)
            vb[half_at(half), :] = projected_by(2, step + 1, half).astype(jnp.bfloat16)

        run_next(columns_in(step + 1, gathered.at[2 * step + 1]), columns_done)
        start, _, run_halves = gather(block_view(2 * step + 2), CHUNKS, 2 * step + 3)
        for half in range(2):
            turn = 2 * (step + 1) + half
            swapped(turn, half)
            for i in every_head:
                score_self(i, step + 1, half)
                score_text(i, half)
            q_col = norms_arrived(turn)
            for i in every_head:
                both = self_part(i, step + 1, half, q_col) + text_part(i, half, q_col)
                pack(both, i, half, gathered.at[2 * step + 2, me])
            start([half])
    orecv[me] = osend[me]
    for k in range(1, n):
        src = lax.rem(me + k, n)
        final_copy(src, src, sibling).wait_recv()
    assemble(orecv, out, 0, span)
    for e, hop, c in text:
        if hop > 0:
            c.wait_send()
        else:
            pl.when(core != e)(c.wait_send)
    middle(core).wait_send()
    for target in range(n):
        pl.when(me != target)(final_copy(target, me, target).wait_send)
    for c in finishes + pending:
        c.wait_send()


def per_device_fused(
    hidden,
    incoming,
    levels,
    mod_table,
    query_weight,
    key_weight,
    value_weight,
    output_weight,
    query_gain,
    key_gain,
    text_keys,
    text_values,
):
    n = lax.axis_size("queue")
    span, width = hidden.shape
    cols = query_weight.shape[1]
    head = width // HEADS
    local = -(-cols // head) * head
    shared = 2 * local - 2 * cols
    step_off = 2 * cols - local
    pair = 2 * cols
    rows = n * span
    text = n * text_keys.shape[0]
    vmem = pl.BlockSpec(memory_space=pltpu.VMEM)
    anywhere = pl.BlockSpec(memory_space=pl.ANY)
    dma = pltpu.SemaphoreType.DMA
    bf16, f32 = jnp.bfloat16, jnp.float32
    most = max(FIRST_CHUNKS, CHUNKS)
    return pl.pallas_call(
        functools.partial(fused_kernel, n, cols),
        out_shape=jax.ShapeDtypeStruct((span, width), hidden.dtype),
        in_specs=[anywhere, vmem, vmem] + [anywhere] * 5 + [vmem] * 2 + [anywhere] * 2,
        out_specs=vmem,
        scratch_shapes=[
            pltpu.VMEM((3, mod_table.shape[0], width), bf16),
            pltpu.VMEM((2, n, width), f32),
            pltpu.VMEM((3 * local, width), bf16),
            pltpu.VMEM((local, width), bf16),
            pltpu.VMEM((n, span, width), bf16),
            pltpu.VMEM((2 * STEPS - 1, n, rows * cols // head, head), bf16),
            pltpu.VMEM((rows + n, width), bf16),
            pltpu.VMEM((rows, 3 * local), f32),
            pltpu.VMEM((n, 3 * local), f32),
            pltpu.VMEM((rows, 128), f32),
            pltpu.VMEM((rows // 2, pair), f32),
            pltpu.VMEM((rows // 2, pair), bf16),
            pltpu.VMEM((rows, local), f32),
            pltpu.VMEM((rows, local), f32),
            pltpu.VMEM((rows, local), f32),
            pltpu.VMEM((rows, local), bf16),
            pltpu.VMEM((rows, local), bf16),
            pltpu.VMEM((rows, local), bf16),
            pltpu.VMEM((local // head, rows, rows), f32),
            pltpu.VMEM((local // head, rows, text), f32),
            pltpu.VMEM((2 * STEPS, 2, rows // 2, shared), bf16),
            pltpu.VMEM((2 * STEPS, 2, rows // 2, shared), bf16),
            pltpu.VMEM((2 * STEPS, 2, rows), f32),
            pltpu.VMEM((2 * STEPS, n, 2, rows), f32),
            pltpu.VMEM((text, step_off), bf16),
            pltpu.VMEM((text, step_off), bf16),
            pltpu.VMEM((2, text, shared), bf16),
            pltpu.VMEM((n, span, local), bf16),
            pltpu.VMEM((n, span, local), bf16),
            dma((9,)),
            dma((2 * STEPS, 15, most)),
            dma((2 * STEPS, n, most)),
            dma((2 * STEPS, n)),
            dma((2 * STEPS, n)),
            dma((2 * STEPS,)),
            dma((2 * STEPS,)),
            dma((2, 2, n // 2)),
            dma((2, n)),
            dma((2, n // 2)),
            dma((n,)),
            dma((2,)),
            dma((n,)),
            dma((n,)),
        ],
        compiler_params=pltpu.CompilerParams(
            collective_id=0, has_side_effects=True, vmem_limit_bytes=60 * 1024 * 1024
        ),
    )(
        hidden,
        incoming,
        levels.reshape(1, n),
        mod_table.transpose(1, 0, 2),
        query_weight.T,
        key_weight.T,
        value_weight.T,
        output_weight.T,
        query_gain.reshape(1, width),
        key_gain.reshape(1, width),
        text_keys,
        text_values,
    )


def fits_fused(count, rows_total, width, groups):
    head = width // HEADS
    cols = width // count
    span = rows_total // (count * groups)
    return (
        count // 4 == 4
        and count % 4 == 0
        and width % 1024 == 0
        and head == 128
        and span == 8
        and (2 * cols) % head == 0
        and cols % head == head // 2
        and cols > head
        and count * span == 128
    )


def choose(mesh):
    def run(hidden, incoming, levels, mod_table, *rest):
        count = lax.axis_size("queue")
        if fits_fused(count, hidden.shape[0] * count, hidden.shape[1], 1):
            return per_device_fused(hidden, incoming, levels, mod_table, *rest)
        return per_device(hidden, incoming, levels, mod_table, *rest)

    return run


def solution(mesh):
    in_specs = (
        P(("groups", "queue"), None),
        P(None, "groups", None),
        P(),
        P(),
        P(None, "queue"),
        P(None, "queue"),
        P(None, "queue"),
        P(None, "queue"),
        P(),
        P(),
        P(("groups", "queue"), None),
        P(("groups", "queue"), None),
    )
    out_specs = P(("groups", "queue"), None)
    return jax.shard_map(
        choose(mesh), mesh=mesh, in_specs=in_specs, out_specs=out_specs, check_vma=False
    )
```

```python
import functools
import math

import jax
import jax.numpy as jnp
from jax import lax
from jax.experimental import pallas as pl
from jax.experimental.pallas import tpu as pltpu
from jax.sharding import PartitionSpec as P

HEADS = 40
STEPS = 2
FIRST_CHUNKS = 2
CHUNKS = 2
HALVES_ORDER = (
    "l10", "s00", "a00", "l20", "a10", "l30", "s10", "b00",
    "l11", "s01", "a20", "l21", "a01", "s20", "a30", "l31",
    "b10", "s30", "a11", "s11", "b20", "b30", "h00", "b01",
    "s21", "a21", "s31", "a31", "b11", "b21", "b31", "h01",
)


def passed_along(value, axis, steps):
    count = lax.axis_size(axis)
    initial, last = (max(0, -steps), min(count, count - steps))
    return lax.ppermute(value, axis, [(source, source + steps) for source in range(initial, last)])


def normalize(values):
    return values * lax.rsqrt(jnp.mean(values * values, axis=-1, keepdims=True) + 1e-06)


def softmax_rounded(scores):
    row_max = jnp.max(scores, axis=-1, keepdims=True)
    weights = jnp.exp(scores - row_max)
    return (weights / jnp.sum(weights, axis=-1, keepdims=True)).astype(jnp.bfloat16)


def pad_slots(values, slot_total):
    missing = slot_total - values.shape[1]
    filler = jnp.zeros((values.shape[0], missing, values.shape[2]), values.dtype)
    return jnp.concatenate([values, filler], axis=1)


def causal_block(queries, keys_all, values_all, span_rows, score_scale):
    total_rows = queries.shape[0]
    block_rows = min(512, total_rows)
    scores = (
        jnp.einsum("qsd,ksd->sqk", queries, keys_all, preferred_element_type=jnp.float32)
        * score_scale
    )
    allowed = (
        jnp.arange(0, block_rows)[:, None] // span_rows
        >= jnp.arange(block_rows)[None, :] // span_rows
    )
    scores = jnp.where(allowed[None], scores, -1e30)
    result = jnp.einsum(
        "sqk,ksd->qsd", softmax_rounded(scores), values_all, preferred_element_type=jnp.float32
    )
    pieces = result.astype(jnp.bfloat16)
    return pieces


def text_attend(queries, text_k, text_v, score_scale):
    scores = (
        jnp.einsum("qsd,tsd->sqt", queries, text_k, preferred_element_type=jnp.float32)
        * score_scale
    )
    return jnp.einsum(
        "sqt,tsd->qsd", softmax_rounded(scores), text_v, preferred_element_type=jnp.float32
    ).astype(jnp.bfloat16)


def per_device(
    hidden,
    incoming,
    levels,
    mod_table,
    query_weight,
    key_weight,
    value_weight,
    output_weight,
    query_gain,
    key_gain,
    text_keys,
    text_values,
):
    own_index = lax.axis_index("queue")
    queue_size = lax.axis_size("queue")
    span_rows, model_width = hidden.shape
    head_size = model_width // HEADS
    score_scale = 1.0 / math.sqrt(head_size)
    slot_total = -(-HEADS // queue_size) * queue_size
    own_level = lax.dynamic_index_in_dim(levels, own_index, 0, keepdims=False)
    modulation = lax.dynamic_index_in_dim(mod_table, own_level, 0, keepdims=False).astype(
        jnp.float32
    )
    stacked_weights = jnp.stack([query_weight, key_weight, value_weight])
    text_local = text_keys.shape[0]
    text_k_slots, text_v_slots = (
        lax.all_to_all(
            pad_slots(text_keys.reshape(text_local, HEADS, head_size), slot_total),
            "queue",
            split_axis=1,
            concat_axis=0,
            tiled=True,
        ),
        lax.all_to_all(
            pad_slots(text_values.reshape(text_local, HEADS, head_size), slot_total),
            "queue",
            split_axis=1,
            concat_axis=0,
            tiled=True,
        ),
    )
    queue_state = hidden
    for section_index in range(STEPS):
        shifted = passed_along(queue_state, "queue", 1)
        queue_state = jnp.where(own_index == 0, incoming[section_index], shifted)
        current = queue_state.astype(jnp.float32)
        modulated = (normalize(current) * (1.0 + modulation[1]) + modulation[0]).astype(
            jnp.bfloat16
        )
        columns = jnp.einsum(
            "rd,cdw->crw",
            lax.all_gather(modulated, "queue", axis=0, tiled=True),
            stacked_weights,
            preferred_element_type=jnp.float32,
        )
        own_rows = lax.all_to_all(
            columns.astype(jnp.bfloat16), "queue", split_axis=1, concat_axis=2, tiled=True
        ).astype(columns.dtype)
        query_heads = (
            (normalize(own_rows[0]) * query_gain)
            .astype(jnp.bfloat16)
            .reshape(span_rows, HEADS, head_size)
        )
        key_heads = (
            (normalize(own_rows[1]) * key_gain)
            .astype(jnp.bfloat16)
            .reshape(span_rows, HEADS, head_size)
        )
        value_heads = own_rows[2].astype(jnp.bfloat16).reshape(span_rows, HEADS, head_size)
        query_slots, key_slots, value_slots = (
            lax.all_to_all(
                pad_slots(query_heads, slot_total), "queue", split_axis=1, concat_axis=0, tiled=True
            ),
            lax.all_to_all(
                pad_slots(key_heads, slot_total), "queue", split_axis=1, concat_axis=0, tiled=True
            ),
            lax.all_to_all(
                pad_slots(value_heads, slot_total), "queue", split_axis=1, concat_axis=0, tiled=True
            ),
        )
        attended_slots = causal_block(query_slots, key_slots, value_slots, span_rows, score_scale)
        crossed_slots = text_attend(query_slots, text_k_slots, text_v_slots, score_scale)
        attended_back, crossed_back = (
            lax.all_to_all(attended_slots, "queue", split_axis=0, concat_axis=1, tiled=True),
            lax.all_to_all(crossed_slots, "queue", split_axis=0, concat_axis=1, tiled=True),
        )
        attended = attended_back[:, :HEADS]
        crossed = crossed_back[:, :HEADS]
        combined = (
            (attended.astype(jnp.float32) + crossed.astype(jnp.float32))
            .astype(jnp.bfloat16)
            .reshape(span_rows, model_width)
        )
        out_columns = jnp.dot(
            lax.all_gather(combined, "queue", axis=0, tiled=True),
            output_weight,
            preferred_element_type=jnp.float32,
        )
        projected = lax.all_to_all(
            out_columns.astype(jnp.bfloat16), "queue", split_axis=0, concat_axis=1, tiled=True
        ).astype(out_columns.dtype)
        queue_state = (current + modulation[2] * projected).astype(jnp.bfloat16)
    return queue_state


def dot_nt(a, b):
    return lax.dot_general(a, b, (((1,), (1,)), ((), ())), preferred_element_type=jnp.float32)


def fused_kernel(
    n,
    cols,
    hidden,
    incoming,
    levels,
    table_hbm,
    wq_hbm,
    wk_hbm,
    wv_hbm,
    wo_hbm,
    q_gain,
    k_gain,
    tkeys,
    tvals,
    out,
    table,
    mods,
    wqkv,
    wo,
    wqkv_t,
    wo_t,
    first,
    gathered,
    full,
    acc,
    shifted,
    squares,
    piece_f32,
    piece_bf16,
    oacc,
    own_cols,
    placed,
    qb,
    kb,
    vb,
    raw_self,
    raw_text,
    xsend,
    xrecv,
    ssend,
    srecv,
    tk,
    tv,
    tmid,
    osend,
    orecv,
    load_sems,
    gsend_sems,
    grecv_sems,
    ssend_sems,
    srecv_sems,
    xsend_sems,
    xrecv_sems,
    tsend_sems,
    trecv_sems,
    msend_sems,
    mrecv_sems,
    msib_sems,
    osend_sems,
    orecv_sems,
):
    me = lax.axis_index("queue")
    span, width = hidden.shape
    head = width // HEADS
    rows = n * span
    pair = 2 * cols
    local = placed.shape[1]
    blocks = gathered.shape[2]
    shared = 2 * local - pair
    step_off = pair - local
    pad = local - cols
    core = lax.rem(me, 2)
    row = lax.rem(me // 2, 2)
    depth = me // 4
    sibling = me + 1 - 2 * core
    start_col = pl.multiple_of((me // 2) * pair + core * step_off, 128)
    mid = pl.multiple_of((1 - core) * step_off, 128)
    mid_start = pl.multiple_of((me // 2) * pair + step_off, 128)
    own_start = pl.multiple_of((me // 2) * pair + core * local, 128)
    trows = tkeys.shape[0]
    scale = 1.0 / math.sqrt(head)

    upper = depth // 2
    folded_depth = depth + upper * (3 - 2 * depth)

    def nth(k):
        x = (folded_depth, 1 - folded_depth, 2, 3)[k]
        return x + upper * (3 - 2 * x)

    along = [4 * nth(k) + 2 * row + core for k in range(4)]
    beside = [4 * nth(k) + 2 * (1 - row) + core for k in range(4)]
    across = me + 2 - 4 * row

    def flip(slot):
        return slot + 1 - 2 * core

    barrier = pltpu.get_barrier_semaphore()
    for k in range(1, n):
        pl.semaphore_signal(
            barrier,
            inc=1,
            device_id={"queue": lax.rem(me + k, n)},
            device_id_type=pl.DeviceIdType.MESH,
        )
    own = pltpu.make_async_copy(hidden, first.at[me], load_sems.at[4])
    own.start()
    own_table = pltpu.make_async_copy(table_hbm, table, load_sems.at[7])
    own_table.start()
    blank = jnp.zeros((pad, width), jnp.bfloat16)
    gap = (1 - core) * cols
    for j in range(3):
        wqkv[pl.ds(pl.multiple_of(j * local + gap, pad), pad), :] = blank
    wo[pl.ds(pl.multiple_of(gap, pad), pad), :] = blank
    loads = [
        pltpu.make_async_copy(
            s, wqkv.at[pl.ds(pl.multiple_of(j * local + core * pad, pad), cols)], load_sems.at[j]
        )
        for j, s in enumerate((wq_hbm, wk_hbm, wv_hbm))
    ]
    loads.append(
        pltpu.make_async_copy(
            wo_hbm, wo.at[pl.ds(pl.multiple_of(core * pad, pad), cols)], load_sems.at[3]
        )
    )
    own_text = [
        pltpu.make_async_copy(
            s.at[:, pl.ds(own_start, step_off)], d.at[pl.ds(me * trows, trows)], load_sems.at[5 + i]
        )
        for i, (s, d) in enumerate(((tkeys, tk), (tvals, tv)))
    ]

    def own_middle(kind):
        return pltpu.make_async_copy(
            (tkeys, tvals)[kind].at[:, pl.ds(mid_start, shared)],
            tmid.at[kind, pl.ds(me * trows, trows)],
            load_sems.at[8],
        )

    for kind in range(2):

        @pl.when(core == kind)
        def _():
            own_middle(kind).start()

    for item in loads + own_text:
        item.start()
    own.wait()
    pl.semaphore_wait(barrier, n - 1)

    pending = []

    def remote(src, dst, send, recv, target):
        return pltpu.make_async_remote_copy(
            src_ref=src,
            dst_ref=dst,
            send_sem=send,
            recv_sem=recv,
            device_id={"queue": target},
            device_id_type=pl.DeviceIdType.MESH,
        )

    finishes = []

    def gather(view, chunks, phase):
        def copy(slot, ch, kind, target):
            return remote(
                view(slot, ch),
                view(slot, ch),
                gsend_sems.at[phase, kind, ch],
                grecv_sems.at[phase, slot, ch],
                target,
            )

        def push(slot, ch, kind, target):
            c = copy(slot, ch, kind, target)
            c.start()
            finishes.append(c)

        def arrived(slot, ch):
            copy(slot, ch, 0, sibling).wait_recv()

        def start(some):
            for ch in some:
                push(me, ch, 0, across)
            for k in range(1, 4):
                for ch in some:
                    push(me, ch, k, along[k])
            for ch in some:
                push(me, ch, 4, sibling)

        def line(k, some):
            for ch in some:
                arrived(along[k], ch)
                push(along[k], ch, 4 + k, across)
                push(along[k], ch, 7 + k, sibling)

        def side(k, some):
            for ch in some:
                arrived(beside[k], ch)
                push(beside[k], ch, 11 + k, sibling)

        def run_rows(on_chip, late):
            every = range(chunks)

            counts = iter(range(n // 2))

            def chip(slot):
                for ch in every:
                    arrived(flip(slot), ch)
                on_chip(slot // 2)
                turn_over_between(next(counts))

            line(1, every)
            chip(me)
            side(0, every)
            chip(along[1])
            line(2, every)
            chip(beside[0])
            side(1, every)
            chip(along[2])
            line(3, every)
            late()
            chip(beside[1])
            side(2, every)
            chip(along[3])
            side(3, every)
            chip(beside[2])
            chip(beside[3])

        def run_halves(on_chip, hook):
            slots = {"a": along, "b": beside}
            opened = set()
            for event in HALVES_ORDER:
                what, k, half = event[0], int(event[1]), int(event[2])
                if what == "l":
                    line(k, [half])
                elif what == "s":
                    side(k, [half])
                elif what == "h":
                    hook(half)
                else:
                    slot = slots[what][k]
                    arrived(flip(slot), half)
                    on_chip(slot // 2, half, half not in opened)
                    opened.add(half)

        return start, run_rows, run_halves

    full_heads = step_off // head
    half_rows = rows // 2
    quarter = half_rows // 2
    half_blocks = blocks // 2
    low = lax.broadcasted_iota(jnp.int32, (quarter, shared), 1) < shared // 2
    owned = (
        lax.broadcasted_iota(jnp.int32, (half_rows, shared), 1) // (shared // 2)
    ) == core

    def head_at(i):
        if i == full_heads:
            return pl.ds(mid, head)
        return pl.ds(pl.multiple_of(core * shared + i * head, 128), head)

    def pack(value, i, half, dst):
        base = half * half_blocks + i * half_rows
        if i < full_heads:
            dst[base : base + half_rows, :] = value.astype(jnp.bfloat16)
        else:
            kept = jnp.where(owned, value, 0.0)
            dst[base : base + quarter, :] = (
                kept[:quarter] + pltpu.roll(kept[quarter:], shared // 2, 1)
            ).astype(jnp.bfloat16)

    def unpack(buf, chip, half, dst):
        a, b = buf.at[2 * chip], buf.at[2 * chip + 1]
        base = half * half_blocks
        for i in range(full_heads):
            part = slice(base + i * half_rows, base + (i + 1) * half_rows)
            dst[:, i * head : (i + 1) * head] = a[part, :].astype(dst.dtype)
            dst[:, local + i * head : local + (i + 1) * head] = b[part, :].astype(dst.dtype)
        base = base + full_heads * half_rows
        fa, fb = (r[base : base + quarter, :].astype(jnp.float32) for r in (a, b))
        dst[:quarter, step_off:local] = jnp.where(low, fa, fb).astype(dst.dtype)
        dst[quarter:, step_off:local] = pltpu.roll(
            jnp.where(low, fb, fa), shared // 2, 1
        ).astype(dst.dtype)

    lane = lax.broadcasted_iota(jnp.int32, (half_rows, local), 1)
    shift = core * pad
    mine = (lane >= shift) & (lane < shift + cols)

    def assemble(buf, dst, base, count):
        for p in range(n // 2):
            a = buf[2 * p, :count]
            b = buf[2 * p + 1, :count]
            at = p * pair
            kept = pl.ds(base, count)
            dst[kept, at : at + step_off] = a[:, :step_off].astype(dst.dtype)
            dst[kept, at + step_off : at + local] = (
                a[:, step_off:].astype(jnp.float32) + b[:, :shared].astype(jnp.float32)
            ).astype(dst.dtype)
            dst[kept, at + local : at + pair] = b[:, shared:].astype(dst.dtype)

    def span_of(block, step):
        return (block + n - STEPS + 1 + step) % n

    def spread(ref, at, step, half):
        first_block = half * n // 2
        return jnp.concatenate(
            [
                jnp.broadcast_to(
                    ref[span_of(i, step) : span_of(i, step) + 1, at], (span, at.size)
                )
                for i in range(first_block, first_block + n // 2)
            ],
            axis=0,
        )

    qg = q_gain[:, pl.ds(start_col, local)]
    kg = k_gain[:, pl.ds(start_col, local)]
    ones = jnp.ones((8, local), jnp.float32)
    def causal(step, half, keys):
        shape = (half_rows, keys)
        moved = half * n // 2 + n - STEPS + 1 + step
        at_row = lax.broadcasted_iota(jnp.int32, shape, 0) // span + moved
        at_col = lax.broadcasted_iota(jnp.int32, shape, 1) // span + n - STEPS + 1 + step
        return lax.rem(at_row, n) >= lax.rem(at_col, n)

    text = []

    def send_text(hops):
        for hop in hops:
            there = lax.rem(me // 2 + hop, n // 2)
            base = pl.multiple_of(there * pair, 128)
            mine_rows = pl.ds(me * trows, trows)
            copies = [
                (
                    e,
                    remote(
                        s.at[:, pl.ds(pl.multiple_of(base + step_off, 128), shared)],
                        tmid.at[e, mine_rows],
                        msend_sems.at[e, hop],
                        mrecv_sems.at[me],
                        2 * there + e,
                    ),
                )
                for e, s in enumerate((tkeys, tvals))
            ] + [
                (
                    e,
                    remote(
                        s.at[:, pl.ds(pl.multiple_of(base + e * local, 128), step_off)],
                        d.at[mine_rows],
                        tsend_sems.at[kind, e, hop],
                        trecv_sems.at[kind, me],
                        2 * there + e,
                    ),
                )
                for kind, (s, d) in enumerate(((tkeys, tk), (tvals, tv)))
                for e in range(2)
            ]
            for e, c in copies:
                if hop > 0:
                    c.start()
                else:
                    pl.when(core != e)(c.start)
                text.append((e, hop, c))

    def text_arrived(kind):
        own_text[kind].wait()
        d = (tk, tv)[kind]
        for k in range(1, n):
            src = lax.rem(me + k, n)
            block = d.at[pl.ds(src * trows, trows)]
            remote(
                block, block, tsend_sems.at[0, 0, 0], trecv_sems.at[kind, src], sibling
            ).wait_recv()

    def middle_arrived():
        own_middle(0).wait()
        for k in range(1, n):
            src = lax.rem(me + k, n)
            block = tmid.at[core, pl.ds(src * trows, trows)]
            remote(block, block, msend_sems.at[0, 0], mrecv_sems.at[src], sibling).wait_recv()

    def middle(kind):
        return remote(
            tmid.at[kind], tmid.at[kind], msib_sems.at[0], msib_sems.at[1], sibling
        )

    def prepare():
        own_table.wait()
        picks = (
            lax.broadcasted_iota(jnp.int32, (table.shape[1], n), 0) == levels[...]
        ).astype(jnp.float32)
        picks = jnp.transpose(picks).astype(jnp.bfloat16)
        drift, gain, gate = (
            jnp.dot(picks, table[kind], preferred_element_type=jnp.float32) for kind in range(3)
        )
        full[rows:, :] = drift.astype(jnp.bfloat16)
        mods[0] = 1.0 + gain
        mods[1] = gate

    fresh_row = lax.broadcasted_iota(jnp.int32, (2 * span, 1024), 0) >= span

    def rows_in(chip):
        place = lax.rem(chip + STEPS // 2, n // 2)
        at = pl.ds(pl.multiple_of(place * 2 * span, 2 * span), 2 * span)
        fresh = fresh_row & (chip == n // 2 - 1)
        later = lax.rem(2 * chip + 2, n)
        total = jnp.zeros((2 * span, 128), jnp.float32)
        for c in range(0, width, 1024):
            block = slice(c, c + 1024)
            new = incoming[0, :, block].astype(jnp.float32)
            x = jnp.concatenate(
                [
                    first[2 * chip, :, block].astype(jnp.float32),
                    first[2 * chip + 1, :, block].astype(jnp.float32),
                ],
                axis=0,
            )
            x = jnp.where(fresh, jnp.concatenate([new, new], axis=0), x)
            gain = jnp.concatenate(
                [
                    jnp.broadcast_to(mods[0, pl.ds(s, 1), block], (span, 1024))
                    for s in (2 * chip + 1, later)
                ],
                axis=0,
            )
            full[at, block] = (x * gain).astype(jnp.bfloat16)
            y = x * x
            for e in range(0, 1024, 128):
                total = total + y[:, e : e + 128]
        squares[at, :] = total

    def turn_over(source, target, lines, chunk):
        at = slice(chunk * pair, (chunk + 1) * pair)
        target[at, lines] = source[lines, at].T

    both_kinds, last_kind = slice(0, 2 * local), slice(2 * local, 3 * local)
    chunk_total = n // 2

    def turn_over_between(count):
        early = chunk_total // 2
        if count == early:
            loads[2].wait()
        if early <= count < early + 2:
            for chunk in range(chunk_total):
                if chunk % 2 == count - early:
                    turn_over(wqkv, wqkv_t, last_kind, chunk)

    def half_at(half):
        return pl.ds(half * half_rows, half_rows)

    def columns_in(step, source):
        def on_chip(chip, half, opening):
            at = pl.ds(pl.multiple_of(chip * pair, 128), pair)
            unpack(source, chip, half, piece_f32)
            if half == 0:
                piece_f32[:span, :] = incoming[step, :, at].astype(jnp.float32)
            x = piece_f32[...]
            piece_bf16[...] = (x * spread(mods.at[0], at, step, half)).astype(jnp.bfloat16)
            y = x * x
            total = y[:, :128]
            for e in range(128, pair, 128):
                total = total + y[:, e : e + 128]
            part = jnp.dot(
                piece_bf16[...], wqkv_t[at, :], preferred_element_type=jnp.float32
            )
            to = half_at(half)
            squares[to, :] = total if opening else squares[to, :] + total
            acc[to, :] = part if opening else acc[to, :] + part

        return on_chip

    def features_in(source):
        def on_chip(chip, half, opening):
            at = pl.ds(pl.multiple_of(chip * pair, 128), pair)
            unpack(source, chip, half, piece_bf16)
            part = jnp.dot(piece_bf16[...], wo_t[at, :], preferred_element_type=jnp.float32)
            to = half_at(half)
            oacc[to, :] = part if opening else oacc[to, :] + part

        return on_chip

    part = width // FIRST_CHUNKS

    def block_view(phase):
        return lambda slot, ch: gathered.at[phase, slot, pl.ds(ch * half_blocks, half_blocks)]

    own_at = pl.ds(start_col, local)

    def norm_copy(turn, k, src, target):
        return remote(
            ssend.at[turn],
            srecv.at[turn, src],
            ssend_sems.at[turn, k],
            srecv_sems.at[turn, src],
            target,
        )

    def swap_copy(turn):
        return remote(
            xsend.at[turn], xrecv.at[turn], xsend_sems.at[turn], xrecv_sems.at[turn], sibling
        )

    def projected_by(j, step, half):
        at = pl.ds(j * local, local)
        to = half_at(half)
        r = lax.rsqrt(
            jnp.sum(squares[to, :], axis=-1, keepdims=True) * (1.0 / width) + 1e-06
        )
        return r * acc[to, at] + spread(shifted, at, step, half)

    def square_sums(value):
        sums = dot_nt(ones, value * value)[0:1]
        return jnp.concatenate([sums, sums], axis=1)

    def launch(step, half):
        turn = 2 * step + half
        to = half_at(half)
        q = projected_by(0, step, half)
        ssend[turn, 0:1] = square_sums(q)
        k_ = projected_by(1, step, half)
        ssend[turn, 1:2] = square_sums(k_)
        for k in range(1, n):
            c = norm_copy(turn, k, me, lax.rem(me + k, n))
            c.start()
            pending.append(c)
        qb[to, :] = (q * qg).astype(jnp.bfloat16)
        kb[to, :] = (k_ * kg).astype(jnp.bfloat16)
        xsend[turn, 0] = qb[to, pl.ds(mid, shared)]
        xsend[turn, 1] = kb[to, pl.ds(mid, shared)]
        swap_copy(turn).start()
        srecv[turn, me] = ssend[turn]

    def swapped(turn, half):
        to = half_at(half)
        swap_copy(turn).wait()
        qb[to, pl.ds(mid, shared)] = qb[to, pl.ds(mid, shared)] + xrecv[turn, 0]
        kb[to, pl.ds(mid, shared)] = kb[to, pl.ds(mid, shared)] + xrecv[turn, 1]

    k_rows = {}

    def norms_arrived(turn):
        for k in range(1, n):
            norm_copy(turn, k, lax.rem(me + k, n), sibling).wait_recv()
        inv = lax.rsqrt(jnp.sum(srecv[turn], axis=0) * (1.0 / width) + 1e-06)
        k_rows[turn] = inv[1:2]
        turned = jnp.transpose(jnp.broadcast_to(inv[0:1], (rows, rows)))
        return turned[:half_rows, 0:1] * scale

    def keys_of(step, half):
        return rows if step == 0 or half == 1 else half_rows

    def score_self(i, step, half):
        keys = keys_of(step, half)
        to = half_at(half)
        raw_self[i, to, :keys] = dot_nt(qb[to, head_at(i)], kb[:keys, head_at(i)])

    def score_text(i, half):
        keys = tk[:, i * head : (i + 1) * head] if i < full_heads else tmid[0]
        to = half_at(half)
        raw_text[i, to, :] = dot_nt(qb[to, head_at(i)], keys)

    low_keys = lax.broadcasted_iota(jnp.int32, (1, rows), 1) < half_rows

    def self_part(i, step, half, q_col):
        keys = keys_of(step, half)
        if keys == rows:
            k_row = jnp.where(low_keys, k_rows[2 * step], k_rows[2 * step + 1])
        else:
            k_row = k_rows[2 * step][:, :keys]
        s = raw_self[i, half_at(half), :keys] * q_col * k_row
        s = jnp.where(causal(step, half, keys), s, -1e30)
        w = jnp.exp(s - jnp.max(s, axis=-1, keepdims=True))
        return jnp.dot(
            w.astype(jnp.bfloat16), vb[:keys, head_at(i)], preferred_element_type=jnp.float32
        ) / jnp.sum(w, axis=-1, keepdims=True)

    def text_part(i, half, q_col):
        values = tv[:, i * head : (i + 1) * head] if i < full_heads else tmid[1]
        t = raw_text[i, half_at(half), :] * q_col
        w = jnp.exp(t - jnp.max(t, axis=-1, keepdims=True))
        return jnp.dot(
            w.astype(jnp.bfloat16), values, preferred_element_type=jnp.float32
        ) / jnp.sum(w, axis=-1, keepdims=True)

    def state_of(step, half):
        to = half_at(half)
        gate = spread(mods.at[1], own_at, step, half)
        return jnp.where(mine, own_cols[to, :] + gate * oacc[to, :], 0.0)

    def final_copy(src, dst, target):
        return remote(
            osend.at[src], orecv.at[dst], osend_sems.at[src], orecv_sems.at[dst], target
        )

    every_head = range(full_heads + 1)
    start, run_rows, _ = gather(
        lambda slot, ch: first.at[slot, :, pl.ds(ch * part, part)], FIRST_CHUNKS, 0
    )
    start(range(FIRST_CHUNKS))
    prepare()
    for item in loads[:2]:
        item.wait()
    for chunk in range(chunk_total):
        turn_over(wqkv, wqkv_t, both_kinds, chunk)
    run_rows(rows_in, lambda: send_text([2, 4, 6, 1, 3, 5, 7, 0]))
    result = jnp.dot(full[...], wqkv_t[:, both_kinds], preferred_element_type=jnp.float32)
    acc[:, : 2 * local] = result[:rows]
    shifted[:, : 2 * local] = result[rows:]
    for half in range(2):
        launch(0, half)
    result = jnp.dot(full[...], wqkv_t[:, last_kind], preferred_element_type=jnp.float32)
    acc[:, 2 * local :] = result[:rows]
    shifted[:, 2 * local :] = result[rows:]
    for i in range(n):
        rows_of = slice(i * span, (i + 1) * span)
        if i == STEPS - 1:
            own_cols[rows_of, :] = incoming[0, :, own_at].astype(jnp.float32)
        else:
            own_cols[rows_of, :] = first[(i - STEPS) % n, :, own_at].astype(jnp.float32)
    for half in range(2):
        vb[half_at(half), :] = projected_by(2, 0, half).astype(jnp.bfloat16)
        swapped(half, half)
    for half in range(2):
        for i in every_head:
            score_self(i, 0, half)
    loads[3].wait()
    for chunk in range(chunk_total):
        turn_over(wo, wo_t, slice(0, local), chunk)
    q_cols = [norms_arrived(half) for half in range(2)]
    for half in range(2):
        for i in every_head:
            placed[half_at(half), i * head : (i + 1) * head] = self_part(i, 0, half, q_cols[half])
    middle_arrived()
    for kind in range(2):
        pl.when(core == kind)(middle(kind).start)
    text_arrived(0)
    for half in range(2):
        for i in range(full_heads):
            score_text(i, half)
    text_arrived(1)
    middle(1 - core).wait_recv()
    start, _, run_halves = gather(block_view(0), CHUNKS, 1)
    for half in range(2):
        score_text(full_heads, half)
        for i in every_head:
            both = placed[half_at(half), i * head : (i + 1) * head] + text_part(
                i, half, q_cols[half]
            )
            pack(both, i, half, gathered.at[0, me])
        start([half])

    for step in range(STEPS):
        last = step == STEPS - 1
        if not last:
            start_next, _, run_next = gather(block_view(2 * step + 1), CHUNKS, 2 * step + 2)

        def features_done(half):
            state = state_of(step, half)
            if last:
                spans = slice(half * n // 2, (half + 1) * n // 2)
                osend[spans] = state.reshape(n // 2, span, local).astype(jnp.bfloat16)
                for target in range(half * n // 2, (half + 1) * n // 2):
                    pl.when(me != target)(final_copy(target, me, target).start)
                return
            placed[half_at(half), :] = state
            for i in every_head:
                pack(placed[half_at(half), head_at(i)], i, half, gathered.at[2 * step + 1, me])
            start_next([half])
            own_cols[half_at(half), :] = state.astype(jnp.bfloat16).astype(jnp.float32)
            if half == 0:
                fresh = slice((STEPS - 2 - step) * span, (STEPS - 1 - step) * span)
                own_cols[fresh, :] = incoming[step + 1, :, own_at].astype(jnp.float32)

        run_halves(features_in(gathered.at[2 * step]), features_done)
        if last:
            break

        def columns_done(half):
            launch(step + 1, half)
            vb[half_at(half), :] = projected_by(2, step + 1, half).astype(jnp.bfloat16)

        run_next(columns_in(step + 1, gathered.at[2 * step + 1]), columns_done)
        start, _, run_halves = gather(block_view(2 * step + 2), CHUNKS, 2 * step + 3)
        for half in range(2):
            turn = 2 * (step + 1) + half
            swapped(turn, half)
            for i in every_head:
                score_self(i, step + 1, half)
                score_text(i, half)
            q_col = norms_arrived(turn)
            for i in every_head:
                both = self_part(i, step + 1, half, q_col) + text_part(i, half, q_col)
                pack(both, i, half, gathered.at[2 * step + 2, me])
            start([half])
    orecv[me] = osend[me]
    for k in range(1, n):
        src = lax.rem(me + k, n)
        final_copy(src, src, sibling).wait_recv()
    assemble(orecv, out, 0, span)
    for e, hop, c in text:
        if hop > 0:
            c.wait_send()
        else:
            pl.when(core != e)(c.wait_send)
    middle(core).wait_send()
    for target in range(n):
        pl.when(me != target)(final_copy(target, me, target).wait_send)
    for c in finishes + pending:
        c.wait_send()


def per_device_fused(
    hidden,
    incoming,
    levels,
    mod_table,
    query_weight,
    key_weight,
    value_weight,
    output_weight,
    query_gain,
    key_gain,
    text_keys,
    text_values,
):
    n = lax.axis_size("queue")
    span, width = hidden.shape
    cols = query_weight.shape[1]
    head = width // HEADS
    local = -(-cols // head) * head
    shared = 2 * local - 2 * cols
    step_off = 2 * cols - local
    pair = 2 * cols
    rows = n * span
    text = n * text_keys.shape[0]
    vmem = pl.BlockSpec(memory_space=pltpu.VMEM)
    anywhere = pl.BlockSpec(memory_space=pl.ANY)
    dma = pltpu.SemaphoreType.DMA
    bf16, f32 = jnp.bfloat16, jnp.float32
    most = max(FIRST_CHUNKS, CHUNKS)
    return pl.pallas_call(
        functools.partial(fused_kernel, n, cols),
        out_shape=jax.ShapeDtypeStruct((span, width), hidden.dtype),
        in_specs=[anywhere, vmem, vmem] + [anywhere] * 5 + [vmem] * 2 + [anywhere] * 2,
        out_specs=vmem,
        scratch_shapes=[
            pltpu.VMEM((3, mod_table.shape[0], width), bf16),
            pltpu.VMEM((2, n, width), f32),
            pltpu.VMEM((3 * local, width), bf16),
            pltpu.VMEM((local, width), bf16),
            pltpu.VMEM((width, 3 * local), bf16),
            pltpu.VMEM((width, local), bf16),
            pltpu.VMEM((n, span, width), bf16),
            pltpu.VMEM((2 * STEPS - 1, n, rows * cols // head, head), bf16),
            pltpu.VMEM((rows + n, width), bf16),
            pltpu.VMEM((rows, 3 * local), f32),
            pltpu.VMEM((n, 3 * local), f32),
            pltpu.VMEM((rows, 128), f32),
            pltpu.VMEM((rows // 2, pair), f32),
            pltpu.VMEM((rows // 2, pair), bf16),
            pltpu.VMEM((rows, local), f32),
            pltpu.VMEM((rows, local), f32),
            pltpu.VMEM((rows, local), f32),
            pltpu.VMEM((rows, local), bf16),
            pltpu.VMEM((rows, local), bf16),
            pltpu.VMEM((rows, local), bf16),
            pltpu.VMEM((local // head, rows, rows), f32),
            pltpu.VMEM((local // head, rows, text), f32),
            pltpu.VMEM((2 * STEPS, 2, rows // 2, shared), bf16),
            pltpu.VMEM((2 * STEPS, 2, rows // 2, shared), bf16),
            pltpu.VMEM((2 * STEPS, 2, rows), f32),
            pltpu.VMEM((2 * STEPS, n, 2, rows), f32),
            pltpu.VMEM((text, step_off), bf16),
            pltpu.VMEM((text, step_off), bf16),
            pltpu.VMEM((2, text, shared), bf16),
            pltpu.VMEM((n, span, local), bf16),
            pltpu.VMEM((n, span, local), bf16),
            dma((9,)),
            dma((2 * STEPS, 15, most)),
            dma((2 * STEPS, n, most)),
            dma((2 * STEPS, n)),
            dma((2 * STEPS, n)),
            dma((2 * STEPS,)),
            dma((2 * STEPS,)),
            dma((2, 2, n // 2)),
            dma((2, n)),
            dma((2, n // 2)),
            dma((n,)),
            dma((2,)),
            dma((n,)),
            dma((n,)),
        ],
        compiler_params=pltpu.CompilerParams(
            collective_id=0, has_side_effects=True, vmem_limit_bytes=60 * 1024 * 1024
        ),
    )(
        hidden,
        incoming,
        levels.reshape(1, n),
        mod_table.transpose(1, 0, 2),
        query_weight.T,
        key_weight.T,
        value_weight.T,
        output_weight.T,
        query_gain.reshape(1, width),
        key_gain.reshape(1, width),
        text_keys,
        text_values,
    )


def fits_fused(count, rows_total, width, groups):
    head = width // HEADS
    cols = width // count
    span = rows_total // (count * groups)
    return (
        count // 4 == 4
        and count % 4 == 0
        and width % 1024 == 0
        and head == 128
        and span == 8
        and (2 * cols) % head == 0
        and cols % head == head // 2
        and cols > head
        and count * span == 128
    )


def choose(mesh):
    def run(hidden, incoming, levels, mod_table, *rest):
        count = lax.axis_size("queue")
        if fits_fused(count, hidden.shape[0] * count, hidden.shape[1], 1):
            return per_device_fused(hidden, incoming, levels, mod_table, *rest)
        return per_device(hidden, incoming, levels, mod_table, *rest)

    return run


def solution(mesh):
    in_specs = (
        P(("groups", "queue"), None),
        P(None, "groups", None),
        P(),
        P(),
        P(None, "queue"),
        P(None, "queue"),
        P(None, "queue"),
        P(None, "queue"),
        P(),
        P(),
        P(("groups", "queue"), None),
        P(("groups", "queue"), None),
    )
    out_specs = P(("groups", "queue"), None)
    return jax.shard_map(
        choose(mesh), mesh=mesh, in_specs=in_specs, out_specs=out_specs, check_vma=False
    )
```

```python
import functools
import math

import jax
import jax.numpy as jnp
from jax import lax
from jax.experimental import pallas as pl
from jax.experimental.pallas import tpu as pltpu
from jax.sharding import PartitionSpec as P

HEADS = 40
STEPS = 2
FIRST_CHUNKS = 2
CHUNKS = 2
HALVES_ORDER = (
    "l10", "s00", "a00", "l20", "a10", "l30", "s10", "b00",
    "l11", "s01", "a20", "l21", "a01", "s20", "a30", "l31",
    "b10", "s30", "a11", "s11", "b20", "b30", "h00", "b01",
    "s21", "a21", "s31", "a31", "b11", "b21", "b31", "h01",
)


def passed_along(value, axis, steps):
    count = lax.axis_size(axis)
    initial, last = (max(0, -steps), min(count, count - steps))
    return lax.ppermute(value, axis, [(source, source + steps) for source in range(initial, last)])


def normalize(values):
    return values * lax.rsqrt(jnp.mean(values * values, axis=-1, keepdims=True) + 1e-06)


def softmax_rounded(scores):
    row_max = jnp.max(scores, axis=-1, keepdims=True)
    weights = jnp.exp(scores - row_max)
    return (weights / jnp.sum(weights, axis=-1, keepdims=True)).astype(jnp.bfloat16)


def pad_slots(values, slot_total):
    missing = slot_total - values.shape[1]
    filler = jnp.zeros((values.shape[0], missing, values.shape[2]), values.dtype)
    return jnp.concatenate([values, filler], axis=1)


def causal_block(queries, keys_all, values_all, span_rows, score_scale):
    total_rows = queries.shape[0]
    block_rows = min(512, total_rows)
    scores = (
        jnp.einsum("qsd,ksd->sqk", queries, keys_all, preferred_element_type=jnp.float32)
        * score_scale
    )
    allowed = (
        jnp.arange(0, block_rows)[:, None] // span_rows
        >= jnp.arange(block_rows)[None, :] // span_rows
    )
    scores = jnp.where(allowed[None], scores, -1e30)
    result = jnp.einsum(
        "sqk,ksd->qsd", softmax_rounded(scores), values_all, preferred_element_type=jnp.float32
    )
    pieces = result.astype(jnp.bfloat16)
    return pieces


def text_attend(queries, text_k, text_v, score_scale):
    scores = (
        jnp.einsum("qsd,tsd->sqt", queries, text_k, preferred_element_type=jnp.float32)
        * score_scale
    )
    return jnp.einsum(
        "sqt,tsd->qsd", softmax_rounded(scores), text_v, preferred_element_type=jnp.float32
    ).astype(jnp.bfloat16)


def per_device(
    hidden,
    incoming,
    levels,
    mod_table,
    query_weight,
    key_weight,
    value_weight,
    output_weight,
    query_gain,
    key_gain,
    text_keys,
    text_values,
):
    own_index = lax.axis_index("queue")
    queue_size = lax.axis_size("queue")
    span_rows, model_width = hidden.shape
    head_size = model_width // HEADS
    score_scale = 1.0 / math.sqrt(head_size)
    slot_total = -(-HEADS // queue_size) * queue_size
    own_level = lax.dynamic_index_in_dim(levels, own_index, 0, keepdims=False)
    modulation = lax.dynamic_index_in_dim(mod_table, own_level, 0, keepdims=False).astype(
        jnp.float32
    )
    stacked_weights = jnp.stack([query_weight, key_weight, value_weight])
    text_local = text_keys.shape[0]
    text_k_slots, text_v_slots = (
        lax.all_to_all(
            pad_slots(text_keys.reshape(text_local, HEADS, head_size), slot_total),
            "queue",
            split_axis=1,
            concat_axis=0,
            tiled=True,
        ),
        lax.all_to_all(
            pad_slots(text_values.reshape(text_local, HEADS, head_size), slot_total),
            "queue",
            split_axis=1,
            concat_axis=0,
            tiled=True,
        ),
    )
    queue_state = hidden
    for section_index in range(STEPS):
        shifted = passed_along(queue_state, "queue", 1)
        queue_state = jnp.where(own_index == 0, incoming[section_index], shifted)
        current = queue_state.astype(jnp.float32)
        modulated = (normalize(current) * (1.0 + modulation[1]) + modulation[0]).astype(
            jnp.bfloat16
        )
        columns = jnp.einsum(
            "rd,cdw->crw",
            lax.all_gather(modulated, "queue", axis=0, tiled=True),
            stacked_weights,
            preferred_element_type=jnp.float32,
        )
        own_rows = lax.all_to_all(
            columns.astype(jnp.bfloat16), "queue", split_axis=1, concat_axis=2, tiled=True
        ).astype(columns.dtype)
        query_heads = (
            (normalize(own_rows[0]) * query_gain)
            .astype(jnp.bfloat16)
            .reshape(span_rows, HEADS, head_size)
        )
        key_heads = (
            (normalize(own_rows[1]) * key_gain)
            .astype(jnp.bfloat16)
            .reshape(span_rows, HEADS, head_size)
        )
        value_heads = own_rows[2].astype(jnp.bfloat16).reshape(span_rows, HEADS, head_size)
        query_slots, key_slots, value_slots = (
            lax.all_to_all(
                pad_slots(query_heads, slot_total), "queue", split_axis=1, concat_axis=0, tiled=True
            ),
            lax.all_to_all(
                pad_slots(key_heads, slot_total), "queue", split_axis=1, concat_axis=0, tiled=True
            ),
            lax.all_to_all(
                pad_slots(value_heads, slot_total), "queue", split_axis=1, concat_axis=0, tiled=True
            ),
        )
        attended_slots = causal_block(query_slots, key_slots, value_slots, span_rows, score_scale)
        crossed_slots = text_attend(query_slots, text_k_slots, text_v_slots, score_scale)
        attended_back, crossed_back = (
            lax.all_to_all(attended_slots, "queue", split_axis=0, concat_axis=1, tiled=True),
            lax.all_to_all(crossed_slots, "queue", split_axis=0, concat_axis=1, tiled=True),
        )
        attended = attended_back[:, :HEADS]
        crossed = crossed_back[:, :HEADS]
        combined = (
            (attended.astype(jnp.float32) + crossed.astype(jnp.float32))
            .astype(jnp.bfloat16)
            .reshape(span_rows, model_width)
        )
        out_columns = jnp.dot(
            lax.all_gather(combined, "queue", axis=0, tiled=True),
            output_weight,
            preferred_element_type=jnp.float32,
        )
        projected = lax.all_to_all(
            out_columns.astype(jnp.bfloat16), "queue", split_axis=0, concat_axis=1, tiled=True
        ).astype(out_columns.dtype)
        queue_state = (current + modulation[2] * projected).astype(jnp.bfloat16)
    return queue_state


def dot_nt(a, b):
    return lax.dot_general(a, b, (((1,), (1,)), ((), ())), preferred_element_type=jnp.float32)


def fused_kernel(
    n,
    cols,
    hidden,
    incoming,
    levels,
    table_hbm,
    wq_hbm,
    wk_hbm,
    wv_hbm,
    wo_hbm,
    q_gain,
    k_gain,
    tkeys,
    tvals,
    out,
    table,
    mods,
    wqkv,
    wo,
    wqkv_t,
    wo_t,
    first,
    gathered,
    full,
    acc,
    shifted,
    squares,
    piece_f32,
    piece_bf16,
    oacc,
    own_cols,
    placed,
    qb,
    kb,
    vb,
    raw_self,
    raw_text,
    xsend,
    xrecv,
    ssend,
    srecv,
    tk,
    tv,
    tmid,
    osend,
    orecv,
    load_sems,
    gsend_sems,
    grecv_sems,
    ssend_sems,
    srecv_sems,
    xsend_sems,
    xrecv_sems,
    tsend_sems,
    trecv_sems,
    msend_sems,
    mrecv_sems,
    msib_sems,
    osend_sems,
    orecv_sems,
):
    me = lax.axis_index("queue")
    span, width = hidden.shape
    head = width // HEADS
    rows = n * span
    pair = 2 * cols
    local = placed.shape[1]
    blocks = gathered.shape[2]
    shared = 2 * local - pair
    step_off = pair - local
    pad = local - cols
    core = lax.rem(me, 2)
    row = lax.rem(me // 2, 2)
    depth = me // 4
    sibling = me + 1 - 2 * core
    start_col = pl.multiple_of((me // 2) * pair + core * step_off, 128)
    mid = pl.multiple_of((1 - core) * step_off, 128)
    mid_start = pl.multiple_of((me // 2) * pair + step_off, 128)
    own_start = pl.multiple_of((me // 2) * pair + core * local, 128)
    trows = tkeys.shape[0]
    scale = 1.0 / math.sqrt(head)

    upper = depth // 2
    folded_depth = depth + upper * (3 - 2 * depth)

    def nth(k):
        x = (folded_depth, 1 - folded_depth, 2, 3)[k]
        return x + upper * (3 - 2 * x)

    along = [4 * nth(k) + 2 * row + core for k in range(4)]
    beside = [4 * nth(k) + 2 * (1 - row) + core for k in range(4)]
    across = me + 2 - 4 * row

    def flip(slot):
        return slot + 1 - 2 * core

    barrier = pltpu.get_barrier_semaphore()
    for k in range(1, n):
        pl.semaphore_signal(
            barrier,
            inc=1,
            device_id={"queue": lax.rem(me + k, n)},
            device_id_type=pl.DeviceIdType.MESH,
        )
    own = pltpu.make_async_copy(hidden, first.at[me], load_sems.at[4])
    own.start()
    own_table = pltpu.make_async_copy(table_hbm, table, load_sems.at[7])
    own_table.start()
    blank = jnp.zeros((pad, width), jnp.bfloat16)
    gap = (1 - core) * cols
    for j in range(3):
        wqkv[pl.ds(pl.multiple_of(j * local + gap, pad), pad), :] = blank
    wo[pl.ds(pl.multiple_of(gap, pad), pad), :] = blank
    loads = [
        pltpu.make_async_copy(
            s, wqkv.at[pl.ds(pl.multiple_of(j * local + core * pad, pad), cols)], load_sems.at[j]
        )
        for j, s in enumerate((wq_hbm, wk_hbm, wv_hbm))
    ]
    loads.append(
        pltpu.make_async_copy(
            wo_hbm, wo.at[pl.ds(pl.multiple_of(core * pad, pad), cols)], load_sems.at[3]
        )
    )
    own_text = [
        pltpu.make_async_copy(
            s.at[:, pl.ds(own_start, step_off)], d.at[pl.ds(me * trows, trows)], load_sems.at[5 + i]
        )
        for i, (s, d) in enumerate(((tkeys, tk), (tvals, tv)))
    ]

    def own_middle(kind):
        return pltpu.make_async_copy(
            (tkeys, tvals)[kind].at[:, pl.ds(mid_start, shared)],
            tmid.at[kind, pl.ds(me * trows, trows)],
            load_sems.at[8],
        )

    for kind in range(2):

        @pl.when(core == kind)
        def _():
            own_middle(kind).start()

    for item in loads + own_text:
        item.start()
    own.wait()
    pl.semaphore_wait(barrier, n - 1)

    pending = []

    def remote(src, dst, send, recv, target):
        return pltpu.make_async_remote_copy(
            src_ref=src,
            dst_ref=dst,
            send_sem=send,
            recv_sem=recv,
            device_id={"queue": target},
            device_id_type=pl.DeviceIdType.MESH,
        )

    finishes = []

    def gather(view, chunks, phase):
        def copy(slot, ch, kind, target):
            return remote(
                view(slot, ch),
                view(slot, ch),
                gsend_sems.at[phase, kind, ch],
                grecv_sems.at[phase, slot, ch],
                target,
            )

        def push(slot, ch, kind, target):
            c = copy(slot, ch, kind, target)
            c.start()
            finishes.append(c)

        def arrived(slot, ch):
            copy(slot, ch, 0, sibling).wait_recv()

        def start(some):
            for ch in some:
                push(me, ch, 0, across)
            for k in range(1, 4):
                for ch in some:
                    push(me, ch, k, along[k])
            for ch in some:
                push(me, ch, 4, sibling)

        def line(k, some):
            for ch in some:
                arrived(along[k], ch)
                push(along[k], ch, 4 + k, across)
                push(along[k], ch, 7 + k, sibling)

        def side(k, some):
            for ch in some:
                arrived(beside[k], ch)
                push(beside[k], ch, 11 + k, sibling)

        def run_rows(on_chip, late):
            every = range(chunks)

            counts = iter(range(n // 2))

            def chip(slot):
                for ch in every:
                    arrived(flip(slot), ch)
                on_chip(slot // 2)
                turn_over_between(next(counts))

            line(1, every)
            side(0, every)
            line(2, every)
            chip(me)
            side(1, every)
            line(3, every)
            late()
            chip(along[1])
            chip(beside[0])
            chip(along[2])
            side(2, every)
            chip(beside[1])
            chip(along[3])
            side(3, every)
            chip(beside[2])
            chip(beside[3])

        def run_halves(on_chip, hook):
            slots = {"a": along, "b": beside}
            opened = set()
            for event in HALVES_ORDER:
                what, k, half = event[0], int(event[1]), int(event[2])
                if what == "l":
                    line(k, [half])
                elif what == "s":
                    side(k, [half])
                elif what == "h":
                    hook(half)
                else:
                    slot = slots[what][k]
                    arrived(flip(slot), half)
                    on_chip(slot // 2, half, half not in opened)
                    opened.add(half)

        return start, run_rows, run_halves

    full_heads = step_off // head
    half_rows = rows // 2
    quarter = half_rows // 2
    half_blocks = blocks // 2
    low = lax.broadcasted_iota(jnp.int32, (quarter, shared), 1) < shared // 2
    owned = (
        lax.broadcasted_iota(jnp.int32, (half_rows, shared), 1) // (shared // 2)
    ) == core

    def head_at(i):
        if i == full_heads:
            return pl.ds(mid, head)
        return pl.ds(pl.multiple_of(core * shared + i * head, 128), head)

    def pack(value, i, half, dst):
        base = half * half_blocks + i * half_rows
        if i < full_heads:
            dst[base : base + half_rows, :] = value.astype(jnp.bfloat16)
        else:
            kept = jnp.where(owned, value, 0.0)
            dst[base : base + quarter, :] = (
                kept[:quarter] + pltpu.roll(kept[quarter:], shared // 2, 1)
            ).astype(jnp.bfloat16)

    def unpack(buf, chip, half, dst):
        a, b = buf.at[2 * chip], buf.at[2 * chip + 1]
        base = half * half_blocks
        for i in range(full_heads):
            part = slice(base + i * half_rows, base + (i + 1) * half_rows)
            dst[:, i * head : (i + 1) * head] = a[part, :].astype(dst.dtype)
            dst[:, local + i * head : local + (i + 1) * head] = b[part, :].astype(dst.dtype)
        base = base + full_heads * half_rows
        fa, fb = (r[base : base + quarter, :].astype(jnp.float32) for r in (a, b))
        dst[:quarter, step_off:local] = jnp.where(low, fa, fb).astype(dst.dtype)
        dst[quarter:, step_off:local] = pltpu.roll(
            jnp.where(low, fb, fa), shared // 2, 1
        ).astype(dst.dtype)

    lane = lax.broadcasted_iota(jnp.int32, (half_rows, local), 1)
    shift = core * pad
    mine = (lane >= shift) & (lane < shift + cols)

    def assemble(buf, dst, base, count):
        for p in range(n // 2):
            a = buf[2 * p, :count]
            b = buf[2 * p + 1, :count]
            at = p * pair
            kept = pl.ds(base, count)
            dst[kept, at : at + step_off] = a[:, :step_off].astype(dst.dtype)
            dst[kept, at + step_off : at + local] = (
                a[:, step_off:].astype(jnp.float32) + b[:, :shared].astype(jnp.float32)
            ).astype(dst.dtype)
            dst[kept, at + local : at + pair] = b[:, shared:].astype(dst.dtype)

    def span_of(block, step):
        return (block + n - STEPS + 1 + step) % n

    def spread(ref, at, step, half):
        first_block = half * n // 2
        return jnp.concatenate(
            [
                jnp.broadcast_to(
                    ref[span_of(i, step) : span_of(i, step) + 1, at], (span, at.size)
                )
                for i in range(first_block, first_block + n // 2)
            ],
            axis=0,
        )

    qg = q_gain[:, pl.ds(start_col, local)]
    kg = k_gain[:, pl.ds(start_col, local)]
    ones = jnp.ones((8, local), jnp.float32)
    def causal(step, half, keys):
        shape = (half_rows, keys)
        moved = half * n // 2 + n - STEPS + 1 + step
        at_row = lax.broadcasted_iota(jnp.int32, shape, 0) // span + moved
        at_col = lax.broadcasted_iota(jnp.int32, shape, 1) // span + n - STEPS + 1 + step
        return lax.rem(at_row, n) >= lax.rem(at_col, n)

    text = []

    def send_text(hops):
        for hop in hops:
            there = lax.rem(me // 2 + hop, n // 2)
            base = pl.multiple_of(there * pair, 128)
            mine_rows = pl.ds(me * trows, trows)
            copies = [
                (
                    e,
                    remote(
                        s.at[:, pl.ds(pl.multiple_of(base + step_off, 128), shared)],
                        tmid.at[e, mine_rows],
                        msend_sems.at[e, hop],
                        mrecv_sems.at[me],
                        2 * there + e,
                    ),
                )
                for e, s in enumerate((tkeys, tvals))
            ] + [
                (
                    e,
                    remote(
                        s.at[:, pl.ds(pl.multiple_of(base + e * local, 128), step_off)],
                        d.at[mine_rows],
                        tsend_sems.at[kind, e, hop],
                        trecv_sems.at[kind, me],
                        2 * there + e,
                    ),
                )
                for kind, (s, d) in enumerate(((tkeys, tk), (tvals, tv)))
                for e in range(2)
            ]
            for e, c in copies:
                if hop > 0:
                    c.start()
                else:
                    pl.when(core != e)(c.start)
                text.append((e, hop, c))

    def text_arrived(kind):
        own_text[kind].wait()
        d = (tk, tv)[kind]
        for k in range(1, n):
            src = lax.rem(me + k, n)
            block = d.at[pl.ds(src * trows, trows)]
            remote(
                block, block, tsend_sems.at[0, 0, 0], trecv_sems.at[kind, src], sibling
            ).wait_recv()

    def middle_arrived():
        own_middle(0).wait()
        for k in range(1, n):
            src = lax.rem(me + k, n)
            block = tmid.at[core, pl.ds(src * trows, trows)]
            remote(block, block, msend_sems.at[0, 0], mrecv_sems.at[src], sibling).wait_recv()

    def middle(kind):
        return remote(
            tmid.at[kind], tmid.at[kind], msib_sems.at[0], msib_sems.at[1], sibling
        )

    def prepare():
        own_table.wait()
        picks = (
            lax.broadcasted_iota(jnp.int32, (table.shape[1], n), 0) == levels[...]
        ).astype(jnp.float32)
        picks = jnp.transpose(picks).astype(jnp.bfloat16)
        drift, gain, gate = (
            jnp.dot(picks, table[kind], preferred_element_type=jnp.float32) for kind in range(3)
        )
        full[rows:, :] = drift.astype(jnp.bfloat16)
        mods[0] = 1.0 + gain
        mods[1] = gate

    fresh_row = lax.broadcasted_iota(jnp.int32, (2 * span, 1024), 0) >= span

    def rows_in(chip):
        place = lax.rem(chip + STEPS // 2, n // 2)
        at = pl.ds(pl.multiple_of(place * 2 * span, 2 * span), 2 * span)
        fresh = fresh_row & (chip == n // 2 - 1)
        later = lax.rem(2 * chip + 2, n)
        total = jnp.zeros((2 * span, 128), jnp.float32)
        for c in range(0, width, 1024):
            block = slice(c, c + 1024)
            new = incoming[0, :, block].astype(jnp.float32)
            x = jnp.concatenate(
                [
                    first[2 * chip, :, block].astype(jnp.float32),
                    first[2 * chip + 1, :, block].astype(jnp.float32),
                ],
                axis=0,
            )
            x = jnp.where(fresh, jnp.concatenate([new, new], axis=0), x)
            gain = jnp.concatenate(
                [
                    jnp.broadcast_to(mods[0, pl.ds(s, 1), block], (span, 1024))
                    for s in (2 * chip + 1, later)
                ],
                axis=0,
            )
            full[at, block] = (x * gain).astype(jnp.bfloat16)
            y = x * x
            for e in range(0, 1024, 128):
                total = total + y[:, e : e + 128]
        squares[at, :] = total

    def turn_over(source, target, lines, chunk):
        at = slice(chunk * pair, (chunk + 1) * pair)
        target[at, lines] = source[lines, at].T

    both_kinds, last_kind = slice(0, 2 * local), slice(2 * local, 3 * local)
    chunk_total = n // 2

    def turn_over_between(count):
        early = chunk_total // 2
        if count == early:
            loads[2].wait()
        if early <= count < early + 2:
            for chunk in range(chunk_total):
                if chunk % 2 == count - early:
                    turn_over(wqkv, wqkv_t, last_kind, chunk)

    def half_at(half):
        return pl.ds(half * half_rows, half_rows)

    def columns_in(step, source):
        def on_chip(chip, half, opening):
            at = pl.ds(pl.multiple_of(chip * pair, 128), pair)
            unpack(source, chip, half, piece_f32)
            if half == 0:
                piece_f32[:span, :] = incoming[step, :, at].astype(jnp.float32)
            x = piece_f32[...]
            piece_bf16[...] = (x * spread(mods.at[0], at, step, half)).astype(jnp.bfloat16)
            y = x * x
            total = y[:, :128]
            for e in range(128, pair, 128):
                total = total + y[:, e : e + 128]
            part = jnp.dot(
                piece_bf16[...], wqkv_t[at, :], preferred_element_type=jnp.float32
            )
            to = half_at(half)
            squares[to, :] = total if opening else squares[to, :] + total
            acc[to, :] = part if opening else acc[to, :] + part

        return on_chip

    def features_in(source):
        def on_chip(chip, half, opening):
            at = pl.ds(pl.multiple_of(chip * pair, 128), pair)
            unpack(source, chip, half, piece_bf16)
            part = jnp.dot(piece_bf16[...], wo_t[at, :], preferred_element_type=jnp.float32)
            to = half_at(half)
            oacc[to, :] = part if opening else oacc[to, :] + part

        return on_chip

    part = width // FIRST_CHUNKS

    def block_view(phase):
        return lambda slot, ch: gathered.at[phase, slot, pl.ds(ch * half_blocks, half_blocks)]

    own_at = pl.ds(start_col, local)

    def norm_copy(turn, k, src, target):
        return remote(
            ssend.at[turn],
            srecv.at[turn, src],
            ssend_sems.at[turn, k],
            srecv_sems.at[turn, src],
            target,
        )

    def swap_copy(turn):
        return remote(
            xsend.at[turn], xrecv.at[turn], xsend_sems.at[turn], xrecv_sems.at[turn], sibling
        )

    def projected_by(j, step, half):
        at = pl.ds(j * local, local)
        to = half_at(half)
        r = lax.rsqrt(
            jnp.sum(squares[to, :], axis=-1, keepdims=True) * (1.0 / width) + 1e-06
        )
        return r * acc[to, at] + spread(shifted, at, step, half)

    def square_sums(value):
        sums = dot_nt(ones, value * value)[0:1]
        return jnp.concatenate([sums, sums], axis=1)

    def launch(step, half):
        turn = 2 * step + half
        to = half_at(half)
        q = projected_by(0, step, half)
        ssend[turn, 0:1] = square_sums(q)
        k_ = projected_by(1, step, half)
        ssend[turn, 1:2] = square_sums(k_)
        for k in range(1, n):
            c = norm_copy(turn, k, me, lax.rem(me + k, n))
            c.start()
            pending.append(c)
        qb[to, :] = (q * qg).astype(jnp.bfloat16)
        kb[to, :] = (k_ * kg).astype(jnp.bfloat16)
        xsend[turn, 0] = qb[to, pl.ds(mid, shared)]
        xsend[turn, 1] = kb[to, pl.ds(mid, shared)]
        swap_copy(turn).start()
        srecv[turn, me] = ssend[turn]

    def swapped(turn, half):
        to = half_at(half)
        swap_copy(turn).wait()
        qb[to, pl.ds(mid, shared)] = qb[to, pl.ds(mid, shared)] + xrecv[turn, 0]
        kb[to, pl.ds(mid, shared)] = kb[to, pl.ds(mid, shared)] + xrecv[turn, 1]

    k_rows = {}

    def norms_arrived(turn):
        for k in range(1, n):
            norm_copy(turn, k, lax.rem(me + k, n), sibling).wait_recv()
        inv = lax.rsqrt(jnp.sum(srecv[turn], axis=0) * (1.0 / width) + 1e-06)
        k_rows[turn] = inv[1:2]
        turned = jnp.transpose(jnp.broadcast_to(inv[0:1], (rows, rows)))
        return turned[:half_rows, 0:1] * scale

    def keys_of(step, half):
        return rows if step == 0 or half == 1 else half_rows

    def score_self(i, step, half):
        keys = keys_of(step, half)
        to = half_at(half)
        raw_self[i, to, :keys] = dot_nt(qb[to, head_at(i)], kb[:keys, head_at(i)])

    def score_text(i, half):
        keys = tk[:, i * head : (i + 1) * head] if i < full_heads else tmid[0]
        to = half_at(half)
        raw_text[i, to, :] = dot_nt(qb[to, head_at(i)], keys)

    low_keys = lax.broadcasted_iota(jnp.int32, (1, rows), 1) < half_rows

    def self_part(i, step, half, q_col):
        keys = keys_of(step, half)
        if keys == rows:
            k_row = jnp.where(low_keys, k_rows[2 * step], k_rows[2 * step + 1])
        else:
            k_row = k_rows[2 * step][:, :keys]
        s = raw_self[i, half_at(half), :keys] * q_col * k_row
        s = jnp.where(causal(step, half, keys), s, -1e30)
        w = jnp.exp(s - jnp.max(s, axis=-1, keepdims=True))
        return jnp.dot(
            w.astype(jnp.bfloat16), vb[:keys, head_at(i)], preferred_element_type=jnp.float32
        ) / jnp.sum(w, axis=-1, keepdims=True)

    def text_part(i, half, q_col):
        values = tv[:, i * head : (i + 1) * head] if i < full_heads else tmid[1]
        t = raw_text[i, half_at(half), :] * q_col
        w = jnp.exp(t - jnp.max(t, axis=-1, keepdims=True))
        return jnp.dot(
            w.astype(jnp.bfloat16), values, preferred_element_type=jnp.float32
        ) / jnp.sum(w, axis=-1, keepdims=True)

    def state_of(step, half):
        to = half_at(half)
        gate = spread(mods.at[1], own_at, step, half)
        return jnp.where(mine, own_cols[to, :] + gate * oacc[to, :], 0.0)

    def final_copy(src, dst, target):
        return remote(
            osend.at[src], orecv.at[dst], osend_sems.at[src], orecv_sems.at[dst], target
        )

    every_head = range(full_heads + 1)
    start, run_rows, _ = gather(
        lambda slot, ch: first.at[slot, :, pl.ds(ch * part, part)], FIRST_CHUNKS, 0
    )
    start(range(FIRST_CHUNKS))
    prepare()
    for item in loads[:2]:
        item.wait()
    for chunk in range(chunk_total):
        turn_over(wqkv, wqkv_t, both_kinds, chunk)
    run_rows(rows_in, lambda: send_text([2, 4, 6, 1, 3, 5, 7, 0]))
    result = jnp.dot(full[...], wqkv_t[:, both_kinds], preferred_element_type=jnp.float32)
    acc[:, : 2 * local] = result[:rows]
    shifted[:, : 2 * local] = result[rows:]
    for half in range(2):
        launch(0, half)
    result = jnp.dot(full[...], wqkv_t[:, last_kind], preferred_element_type=jnp.float32)
    acc[:, 2 * local :] = result[:rows]
    shifted[:, 2 * local :] = result[rows:]
    for i in range(n):
        rows_of = slice(i * span, (i + 1) * span)
        if i == STEPS - 1:
            own_cols[rows_of, :] = incoming[0, :, own_at].astype(jnp.float32)
        else:
            own_cols[rows_of, :] = first[(i - STEPS) % n, :, own_at].astype(jnp.float32)
    for half in range(2):
        vb[half_at(half), :] = projected_by(2, 0, half).astype(jnp.bfloat16)
        swapped(half, half)
    for half in range(2):
        for i in every_head:
            score_self(i, 0, half)
    loads[3].wait()
    for chunk in range(chunk_total):
        turn_over(wo, wo_t, slice(0, local), chunk)
    q_cols = [norms_arrived(half) for half in range(2)]
    for half in range(2):
        for i in every_head:
            placed[half_at(half), i * head : (i + 1) * head] = self_part(i, 0, half, q_cols[half])
    middle_arrived()
    for kind in range(2):
        pl.when(core == kind)(middle(kind).start)
    text_arrived(0)
    for half in range(2):
        for i in range(full_heads):
            score_text(i, half)
    text_arrived(1)
    middle(1 - core).wait_recv()
    start, _, run_halves = gather(block_view(0), CHUNKS, 1)
    for half in range(2):
        score_text(full_heads, half)
        for i in every_head:
            both = placed[half_at(half), i * head : (i + 1) * head] + text_part(
                i, half, q_cols[half]
            )
            pack(both, i, half, gathered.at[0, me])
        start([half])

    for step in range(STEPS):
        last = step == STEPS - 1
        if not last:
            start_next, _, run_next = gather(block_view(2 * step + 1), CHUNKS, 2 * step + 2)

        def features_done(half):
            state = state_of(step, half)
            if last:
                spans = slice(half * n // 2, (half + 1) * n // 2)
                osend[spans] = state.reshape(n // 2, span, local).astype(jnp.bfloat16)
                for target in range(half * n // 2, (half + 1) * n // 2):
                    pl.when(me != target)(final_copy(target, me, target).start)
                return
            placed[half_at(half), :] = state
            for i in every_head:
                pack(placed[half_at(half), head_at(i)], i, half, gathered.at[2 * step + 1, me])
            start_next([half])
            own_cols[half_at(half), :] = state.astype(jnp.bfloat16).astype(jnp.float32)
            if half == 0:
                fresh = slice((STEPS - 2 - step) * span, (STEPS - 1 - step) * span)
                own_cols[fresh, :] = incoming[step + 1, :, own_at].astype(jnp.float32)

        run_halves(features_in(gathered.at[2 * step]), features_done)
        if last:
            break

        def columns_done(half):
            launch(step + 1, half)
            vb[half_at(half), :] = projected_by(2, step + 1, half).astype(jnp.bfloat16)

        run_next(columns_in(step + 1, gathered.at[2 * step + 1]), columns_done)
        start, _, run_halves = gather(block_view(2 * step + 2), CHUNKS, 2 * step + 3)
        for half in range(2):
            turn = 2 * (step + 1) + half
            swapped(turn, half)
            for i in every_head:
                score_self(i, step + 1, half)
                score_text(i, half)
            q_col = norms_arrived(turn)
            for i in every_head:
                both = self_part(i, step + 1, half, q_col) + text_part(i, half, q_col)
                pack(both, i, half, gathered.at[2 * step + 2, me])
            start([half])
    orecv[me] = osend[me]
    for k in range(1, n):
        src = lax.rem(me + k, n)
        final_copy(src, src, sibling).wait_recv()
    assemble(orecv, out, 0, span)
    for e, hop, c in text:
        if hop > 0:
            c.wait_send()
        else:
            pl.when(core != e)(c.wait_send)
    middle(core).wait_send()
    for target in range(n):
        pl.when(me != target)(final_copy(target, me, target).wait_send)
    for c in finishes + pending:
        c.wait_send()


def per_device_fused(
    hidden,
    incoming,
    levels,
    mod_table,
    query_weight,
    key_weight,
    value_weight,
    output_weight,
    query_gain,
    key_gain,
    text_keys,
    text_values,
):
    n = lax.axis_size("queue")
    span, width = hidden.shape
    cols = query_weight.shape[1]
    head = width // HEADS
    local = -(-cols // head) * head
    shared = 2 * local - 2 * cols
    step_off = 2 * cols - local
    pair = 2 * cols
    rows = n * span
    text = n * text_keys.shape[0]
    vmem = pl.BlockSpec(memory_space=pltpu.VMEM)
    anywhere = pl.BlockSpec(memory_space=pl.ANY)
    dma = pltpu.SemaphoreType.DMA
    bf16, f32 = jnp.bfloat16, jnp.float32
    most = max(FIRST_CHUNKS, CHUNKS)
    return pl.pallas_call(
        functools.partial(fused_kernel, n, cols),
        out_shape=jax.ShapeDtypeStruct((span, width), hidden.dtype),
        in_specs=[anywhere, vmem, vmem] + [anywhere] * 5 + [vmem] * 2 + [anywhere] * 2,
        out_specs=vmem,
        scratch_shapes=[
            pltpu.VMEM((3, mod_table.shape[0], width), bf16),
            pltpu.VMEM((2, n, width), f32),
            pltpu.VMEM((3 * local, width), bf16),
            pltpu.VMEM((local, width), bf16),
            pltpu.VMEM((width, 3 * local), bf16),
            pltpu.VMEM((width, local), bf16),
            pltpu.VMEM((n, span, width), bf16),
            pltpu.VMEM((2 * STEPS - 1, n, rows * cols // head, head), bf16),
            pltpu.VMEM((rows + n, width), bf16),
            pltpu.VMEM((rows, 3 * local), f32),
            pltpu.VMEM((n, 3 * local), f32),
            pltpu.VMEM((rows, 128), f32),
            pltpu.VMEM((rows // 2, pair), f32),
            pltpu.VMEM((rows // 2, pair), bf16),
            pltpu.VMEM((rows, local), f32),
            pltpu.VMEM((rows, local), f32),
            pltpu.VMEM((rows, local), f32),
            pltpu.VMEM((rows, local), bf16),
            pltpu.VMEM((rows, local), bf16),
            pltpu.VMEM((rows, local), bf16),
            pltpu.VMEM((local // head, rows, rows), f32),
            pltpu.VMEM((local // head, rows, text), f32),
            pltpu.VMEM((2 * STEPS, 2, rows // 2, shared), bf16),
            pltpu.VMEM((2 * STEPS, 2, rows // 2, shared), bf16),
            pltpu.VMEM((2 * STEPS, 2, rows), f32),
            pltpu.VMEM((2 * STEPS, n, 2, rows), f32),
            pltpu.VMEM((text, step_off), bf16),
            pltpu.VMEM((text, step_off), bf16),
            pltpu.VMEM((2, text, shared), bf16),
            pltpu.VMEM((n, span, local), bf16),
            pltpu.VMEM((n, span, local), bf16),
            dma((9,)),
            dma((2 * STEPS, 15, most)),
            dma((2 * STEPS, n, most)),
            dma((2 * STEPS, n)),
            dma((2 * STEPS, n)),
            dma((2 * STEPS,)),
            dma((2 * STEPS,)),
            dma((2, 2, n // 2)),
            dma((2, n)),
            dma((2, n // 2)),
            dma((n,)),
            dma((2,)),
            dma((n,)),
            dma((n,)),
        ],
        compiler_params=pltpu.CompilerParams(
            collective_id=0, has_side_effects=True, vmem_limit_bytes=60 * 1024 * 1024
        ),
    )(
        hidden,
        incoming,
        levels.reshape(1, n),
        mod_table.transpose(1, 0, 2),
        query_weight.T,
        key_weight.T,
        value_weight.T,
        output_weight.T,
        query_gain.reshape(1, width),
        key_gain.reshape(1, width),
        text_keys,
        text_values,
    )


def fits_fused(count, rows_total, width, groups):
    head = width // HEADS
    cols = width // count
    span = rows_total // (count * groups)
    return (
        count // 4 == 4
        and count % 4 == 0
        and width % 1024 == 0
        and head == 128
        and span == 8
        and (2 * cols) % head == 0
        and cols % head == head // 2
        and cols > head
        and count * span == 128
    )


def choose(mesh):
    def run(hidden, incoming, levels, mod_table, *rest):
        count = lax.axis_size("queue")
        if fits_fused(count, hidden.shape[0] * count, hidden.shape[1], 1):
            return per_device_fused(hidden, incoming, levels, mod_table, *rest)
        return per_device(hidden, incoming, levels, mod_table, *rest)

    return run


def solution(mesh):
    in_specs = (
        P(("groups", "queue"), None),
        P(None, "groups", None),
        P(),
        P(),
        P(None, "queue"),
        P(None, "queue"),
        P(None, "queue"),
        P(None, "queue"),
        P(),
        P(),
        P(("groups", "queue"), None),
        P(("groups", "queue"), None),
    )
    out_specs = P(("groups", "queue"), None)
    return jax.shard_map(
        choose(mesh), mesh=mesh, in_specs=in_specs, out_specs=out_specs, check_vma=False
    )
```
